128 devices in a mesh: lat: 8 (over z, core), lon: 16 (over x, y).
Axes of the slice: x: 4, y: 4, z: 4, core: 2. Of those that a mesh axis runs over, the one named last changes fastest.
Arguments:
- tracers: float32 [2, 48, 1024, 2048], P(None, None, 'lat', 'lon'), may hold values from -6 to 6
- east_courant: float32 [48, 1024, 2048], P(None, 'lat', 'lon'), may hold values from -0.4 to 0.4
- north_courant: float32 [48, 1024, 2048], P(None, 'lat', 'lon'), may hold values from -0.4 to 0.4
- diffusivity: float32 [48, 1024, 2048], P(None, 'lat', 'lon'), may hold values from 0.05 to 20
- land_sea: int32 [1024, 2048], P('lat', 'lon'), may hold values 0 or 1
- fluxes: float32 [6, 1048576], P(None, ('lat', 'lon')), may hold values from -6 to 6
- source_cell: int32 [128, 4, 6144], P(('lat', 'lon')), may hold values from 0 to 8191, as said below
- link_weight: float32 [128, 4, 6144], P(('lat', 'lon')), may hold values from 0.05 to 0.3
- target_cell: int32 [128, 4, 6144], P(('lat', 'lon')), may hold values from 0 to 16383, as said below
Outputs:
- stepped: float32 [2, 48, 1024, 2048], P(None, None, 'lat', 'lon')
The draws below stay inside these ranges and needn't reach their ends.
Inputs may be any that keep to these rules, and one draw needn't show every extreme that they name: source_cell[s, n, c] lies in n * 2048 to (n+1) * 2048 - 1; several links may name the same cells. target_cell[d, n, c] has its row in (1 - n // 2) * 64 to that plus 128 // 2 - 1 and its column in (1 - n % 2) * 64 to that plus 128 // 2 - 1.
All inputs are finite; a program needn't handle non-finite values. No bound on the sum of `land_sea` on one device may be relied on, other than what follows from the above.
Results may differ from the reference program's by a relative error of at most 0.00005.
Values sent between devices are 32-bit elements; how exact they have to be, the bound alone decides.
A program may use at most 192 MiB of HBM per device.

```python
import math
import jax
import jax.numpy as jnp

FIELDS = 6
LEVELS = 48
CLAT = 128
CLON = 128
ATM_DEV = 8192
CAP = 6144
NLAT = 1024
NLON = 2048
ATM_CELLS = 1048576
N_LAT = 8
N_LON = 16
DEVICES = 128


def draw_source_cell(key, part):
    quarter = ATM_DEV // 4
    offset = jax.random.randint(key, (DEVICES, 4, CAP), 0, quarter, dtype=jnp.int32)
    base = (jnp.arange(4, dtype=jnp.int32) * quarter)[None, :, None]
    cells = offset + base
    cells = cells.at[:, 3, 0].set(ATM_DEV - 1)
    cells = cells.at[:, 0, 0].set(0)
    return cells


def draw_target_cell(key, part):
    half_rows = CLAT // 2
    half_cols = CLON // 2
    row_key = jax.random.fold_in(key, 11)
    col_key = jax.random.fold_in(key, 23)
    rows = jax.random.randint(row_key, (DEVICES, 4, CAP), 0, half_rows, dtype=jnp.int32)
    cols = jax.random.randint(col_key, (DEVICES, 4, CAP), 0, half_cols, dtype=jnp.int32)
    intersection = jnp.arange(4, dtype=jnp.int32)[None, :, None]
    rows = rows + (1 - intersection // 2) * half_rows
    cols = cols + (1 - intersection % 2) * half_cols
    cells = rows * CLON + cols
    cells = cells.at[:, 0, 0].set(CLAT * CLON - 1)
    cells = cells.at[:, 3, 0].set(0)
    return cells


def place_ends(array, own_key, least, largest):
    shape = array.shape
    index_at = [jax.random.randint(jax.random.fold_in(own_key, axis), (), 0, shape[axis]) for axis in range(len(shape))]
    array = array.at[tuple(index_at)].set(least)
    longest = shape.index(max(shape))
    index_at[longest] = (index_at[longest] + 1) % shape[longest]
    return array.at[tuple(index_at)].set(largest)


def steps_of(own_key, extent, shards, smallest, top_value):
    factor_of, own = 1.0, jax.random.fold_in(own_key, 6)
    for axis_at, blocks in shards:
        draws = jnp.exp(jax.random.uniform(jax.random.fold_in(own, axis_at), (blocks,), jnp.float32, smallest / len(shards), top_value / len(shards)))
        factor_of = factor_of * jnp.repeat(draws, extent[axis_at] // blocks).reshape([-1 if axis == axis_at else 1 for axis in range(len(extent))])
    return factor_of


def normal_values(key, extent, deviation, bound, cuts=(), held_as=jnp.bfloat16):
    drawn = jax.random.normal(key, extent, jnp.float32) * deviation
    if len(cuts) > 0:
        drawn = steps_of(key, extent, cuts, -0.22, 0.18) * drawn
    return jnp.clip(drawn, min=-bound, max=bound).astype(held_as)


def setup_inputs(seed: int = 0) -> dict:
    keys = jax.random.split(jax.random.key(seed), 10)
    return {
        "tracers": normal_values(keys[0], (2, LEVELS, NLAT, NLON), 1.0, 6.0, ((2, 8), (3, 16)), jnp.float32),
        "east_courant": jnp.clip(jax.random.uniform(keys[1], (LEVELS, NLAT, NLON), jnp.float32, -0.4, 0.4) * steps_of(keys[1], (LEVELS, NLAT, NLON), ((1, 8), (2, 16)), -0.4, 0.0), -0.4, 0.4),
        "north_courant": jnp.clip(jax.random.uniform(keys[2], (LEVELS, NLAT, NLON), jnp.float32, -0.4, 0.4) * steps_of(keys[2], (LEVELS, NLAT, NLON), ((1, 8), (2, 16)), -0.4, 0.0), -0.4, 0.4),
        "diffusivity": jnp.clip(jnp.exp(math.log(20.0) - 5.9914645 * jax.random.uniform(keys[3], (LEVELS, NLAT, NLON), jnp.float32) ** steps_of(keys[3], (LEVELS, NLAT, NLON), ((1, 8), (2, 16)), -0.2, 0.2)), 0.05, 20.0),
        "land_sea": place_ends((jax.random.randint(keys[4], (NLAT, NLON), 0, 4) < 3).astype(jnp.int32), jax.random.fold_in(keys[4], 1), 0, 1),
        "fluxes": normal_values(keys[5], (FIELDS, ATM_CELLS), 1.0, 6.0, ((1, 128),), jnp.float32),
        "source_cell": draw_source_cell(jax.random.fold_in(keys[9], 71), 0),
        "link_weight": jnp.clip(0.05 + 0.25 * jax.random.uniform(keys[7], (DEVICES, 4, CAP), jnp.float32) ** steps_of(keys[7], (DEVICES, 4, CAP), ((0, 128),), -0.2, 0.2), 0.05, 0.3),
        "target_cell": draw_target_cell(jax.random.fold_in(keys[9], 71), 0),
    }


def face(lower_two, lower_one, upper_one, upper_two):
    return (7.0 * (lower_one + upper_one) - (lower_two + upper_two)) / 12.0

def column_solve(right_side, mixing):
    levels = mixing.shape[0]
    above = jnp.zeros_like(mixing[0])
    prior_upper = jnp.zeros_like(mixing[0])
    prior_value = jnp.zeros_like(right_side[:, 0])
    uppers = []
    values = []
    for level in range(levels):
        below = mixing[level]
        pivot = 1.0 + above + below + above * prior_upper
        value = (right_side[:, level] + above * prior_value) / pivot
        prior_upper = -below / pivot
        prior_value = value
        uppers.append(prior_upper)
        values.append(value)
        above = below
    result = [None] * levels
    result[levels - 1] = values[levels - 1]
    for level in range(levels - 2, -1, -1):
        result[level] = values[level] - uppers[level] * result[level + 1]
    return jnp.stack(result, 1)

def forcing(advected, surface, diffusivity):
    levels = advected.shape[1]
    depth = jnp.arange(levels, dtype=jnp.float32)
    absorb = jnp.exp(-4.0 * depth / levels) - jnp.exp(-4.0 * (depth + 1.0) / levels)
    decay = jnp.exp(-4.0 * depth / levels)
    keep = (jnp.arange(levels) < levels - 1).astype(jnp.float32)
    heat_part = advected[0] + 0.5 * surface[2][None] * absorb[:, None, None]
    heat_part = heat_part.at[0].add(0.5 * surface[0])
    salt_part = advected[1].at[0].add(0.5 * (surface[1] + surface[5]))
    forced = jnp.stack([heat_part, salt_part], 0)
    stress = jnp.sqrt(surface[3] * surface[3] + surface[4] * surface[4])
    mixing = (diffusivity + 2.0 * stress[None] * decay[:, None, None]) * keep[:, None, None]
    return (forced, mixing)

def reference(tracers, east_courant, north_courant, diffusivity, land_sea, fluxes, source_cell, link_weight, target_cell):
    devices = N_LAT * N_LON
    owner = jnp.arange(devices, dtype=jnp.int32)[:, None]
    intersection = jnp.arange(4, dtype=jnp.int32)[None, :]
    lat_off = intersection // 2
    lon_off = intersection % 2
    owner_lat = owner // N_LON
    owner_lon = owner % N_LON
    sender_lat = owner_lat - lat_off
    exists = (sender_lat >= 0).astype(jnp.float32)
    sender = sender_lat % N_LAT * N_LON + (owner_lon - lon_off) % N_LON
    picked_cell = source_cell[sender, intersection]
    picked_weight = link_weight[sender, intersection] * exists[:, :, None]
    global_cell = (picked_cell + (sender * ATM_DEV)[:, :, None]).reshape(-1)
    values = jnp.take(fluxes, global_cell, axis=1) * picked_weight.reshape(-1)[None]
    row = (owner_lat * CLAT)[:, :, None] + target_cell // CLON
    col = (owner_lon * CLON)[:, :, None] + target_cell % CLON
    flat = (row * NLON + col).reshape(-1)
    surface = jnp.zeros((FIELDS, NLAT * NLON), jnp.float32).at[:, flat].add(values)
    surface = surface.reshape(FIELDS, NLAT, NLON)
    east_val = face(jnp.roll(tracers, 1, 3), tracers, jnp.roll(tracers, -1, 3), jnp.roll(tracers, -2, 3))
    east_flux = east_courant[None] * east_val
    west_flux = jnp.roll(east_flux, 1, 3)
    padded = jnp.pad(tracers, ((0, 0), (0, 0), (2, 2), (0, 0)))
    north_val = face(padded[:, :, 1:NLAT + 1], padded[:, :, 2:NLAT + 2], padded[:, :, 3:NLAT + 3], padded[:, :, 4:NLAT + 4])
    north_flux = north_courant[None] * north_val
    south_flux = jnp.concatenate([jnp.zeros_like(north_flux[:, :, :1]), north_flux[:, :, :-1]], 2)
    advected = tracers - (east_flux - west_flux) - (north_flux - south_flux)
    forced, mixing = forcing(advected, surface, diffusivity)
    solved = column_solve(forced, mixing)
    return jnp.where((land_sea == 1)[None, None], solved, tracers)
```

```python
import math
import jax, jax.numpy as jnp
import numpy as np
from jax import lax
from jax.experimental import pallas as pl
from jax.experimental.pallas import tpu as pltpu
from jax.sharding import PartitionSpec as P

LEVELS = 48
HALF = 24
R = 32
G = 8
PAD = 8


def stencil_weights():
    cols = 128
    main = np.zeros((cols, 2 * cols), np.float32)
    for i in range(cols):
        for off, w in ((-1, -1), (0, 7), (1, 7), (2, -1)):
            if 0 <= i + off < cols:
                main[i + off, i] = w
        for off, w in ((-2, -1), (-1, 7), (0, 7), (1, -1)):
            if 0 <= i + off < cols:
                main[i + off, cols + i] = w
    halves = []
    for half in range(2):
        edge = np.zeros((cols, 2 * cols), np.float32)
        order = (-2, -1, 128, 129) if half == 0 else (128, 129, -2, -1)
        for lane in range(cols):
            p = order[lane % 4]
            for i in range(cols):
                edge[lane, i] = {-1: -1, 0: 7, 1: 7, 2: -1}.get(p - i, 0)
                edge[lane, cols + i] = {-2: -1, -1: 7, 0: 7, 1: -1}.get(p - i, 0)
        halves.append(np.concatenate([main, main, edge, edge], 0))
    return jnp.asarray(np.stack(halves), jnp.bfloat16)


def two_pieces(x):
    high = x.astype(jnp.bfloat16)
    return high, (x - high.astype(jnp.float32)).astype(jnp.bfloat16)


def column_kernel(tr_hbm, ec_hbm, nc_hbm, df_hbm, w_ref, land_ref, surf_ref, pe_ref, pw_ref, south_ref, north_ref, ncs_ref,
                  out_hbm, T, EC, NC, DF, C, OUT, H, X, S, FN, in_sem, out_sem):
    rows, cols = 128, 128
    blocks = rows // R

    def loads(b):
        r = pl.multiple_of(b * R, R)
        return [
            pltpu.make_async_copy(tr_hbm.at[:, :, pl.ds(r, R), :], T.at[:, :, pl.ds(r + PAD, R), :], in_sem.at[b, 0]),
            pltpu.make_async_copy(ec_hbm.at[:, pl.ds(r, R), :], EC.at[:, pl.ds(r, R), :], in_sem.at[b, 1]),
            pltpu.make_async_copy(nc_hbm.at[:, pl.ds(r, R), :], NC.at[:, pl.ds(r, R), :], in_sem.at[b, 2]),
            pltpu.make_async_copy(df_hbm.at[:, pl.ds(r, R), :], DF.at[:, pl.ds(r, R), :], in_sem.at[b, 3]),
        ]

    def start(b, carry):
        for c in loads(b):
            c.start()
        return carry

    lax.fori_loop(0, blocks, start, 0)

    lane = lax.broadcasted_iota(jnp.int32, (rows, cols), 1)
    low = lane % 4 < 2
    for t in range(2):
        pe, pw = pe_ref[t], pw_ref[t]
        for half in range(2):
            h = jnp.where(low, pw, pe) if half == 0 else jnp.where(low, pe, pw)
            H[t, half, 0], H[t, half, 1] = two_pieces(h)

    for c in loads(0):
        c.wait()

    def edges(k, carry):
        for t in range(2):
            T[t, k, PAD - 2:PAD, :] = south_ref[t, k]
            T[t, k, PAD + rows:PAD + rows + 2, :] = north_ref[t, k]
            s = T[t, k, PAD - 2:PAD - 1, :] + T[t, k, PAD + 1:PAD + 2, :]
            m = T[t, k, PAD - 1:PAD, :] + T[t, k, PAD:PAD + 1, :]
            FN[t, k, PAD - 1:PAD, :] = ncs_ref[k] * (7.0 * m - s)
        return carry

    lax.fori_loop(0, LEVELS, edges, 0)

    def block(b, carry):
        @pl.when(b + 1 < blocks)
        def _():
            for c in loads(b + 1):
                c.wait()

        r = pl.multiple_of(b * R, R)
        rr = pl.ds(r, R)
        lane = lax.broadcasted_iota(jnp.int32, (R, cols), 1)
        first = lane == 0
        stress = 2.0 * jnp.sqrt(surf_ref[3, rr, :] * surf_ref[3, rr, :] + surf_ref[4, rr, :] * surf_ref[4, rr, :])

        for half in range(2):
            def group(q, carry):
                for u in range(G):
                    j = q * G + u
                    k = half * HALF + j
                    here = (lane + 2 * half) % cols // 4 == j
                    for t in range(2):
                        x = T[t, k, pl.ds(r + PAD, R), :]
                        at = pl.ds((u * 2 + t) * R, R)
                        X[at, 0:cols], X[at, cols:2 * cols] = two_pieces(x)
                        for p in range(2):
                            h = H[t, half, p, rr, :]
                            X[at, (2 + p) * cols:(3 + p) * cols] = jnp.where(here, h, jnp.zeros_like(h))
                S[...] = jnp.dot(X[...], w_ref[half], preferred_element_type=jnp.float32)
                for u in range(G):
                    j = q * G + u
                    k = half * HALF + j
                    ce = EC[k, rr, :]
                    cn = NC[k, rr, :]
                    hec = pltpu.roll(pw_ref[half, rr, :], cols - 96 - j, 1)
                    cw = jnp.where(first, hec, pltpu.roll(ce, 1, 1))
                    for t in range(2):
                        at = pl.ds((u * 2 + t) * R, R)
                        x = T[t, k, pl.ds(r + PAD, R), :]
                        n1 = T[t, k, pl.ds(r + PAD + 1, R), :]
                        n2 = T[t, k, pl.ds(r + PAD + 2, R), :]
                        s1 = T[t, k, pl.ds(r + PAD - 1, R), :]
                        fn = cn * (7.0 * (x + n1) - (s1 + n2))
                        FN[t, k, pl.ds(r + PAD, R), :] = fn
                        fs = FN[t, k, pl.ds(r + PAD - 1, R), :]
                        div = (ce * S[at, 0:cols] - cw * S[at, cols:2 * cols]) + (fn - fs)
                        OUT[t, k, rr, :] = x - div * (1.0 / 12.0)
                return carry

            lax.fori_loop(0, HALF // G, group, 0)

        heat = 0.5 * surf_ref[2, rr, :]
        tops = [0.5 * surf_ref[0, rr, :], 0.5 * surf_ref[1, rr, :]]
        above = None
        cprev = None
        vprev = [None, None]
        for k in range(LEVELS):
            if k < LEVELS - 1:
                below = DF[k, rr, :] + stress * math.exp(-4.0 * k / LEVELS)
            absorb = math.exp(-4.0 * k / LEVELS) - math.exp(-4.0 * (k + 1) / LEVELS)
            adv = [OUT[0, k, rr, :] + heat * absorb, OUT[1, k, rr, :]]
            if k == 0:
                adv[0] = adv[0] + tops[0]
                adv[1] = adv[1] + tops[1]
                inv = 1.0 / (1.0 + below)
                v = [adv[0] * inv, adv[1] * inv]
            else:
                pivot = 1.0 + above * (1.0 - cprev)
                if k < LEVELS - 1:
                    pivot = pivot + below
                inv = 1.0 / pivot
                v = [(adv[t] + above * vprev[t]) * inv for t in range(2)]
            if k < LEVELS - 1:
                cprev = below * inv
                C[k] = cprev
                above = below
                for t in range(2):
                    OUT[t, k, rr, :] = v[t]
            vprev = v
        sea = land_ref[rr, :] == 1
        x = vprev
        for k in range(LEVELS - 1, -1, -1):
            if k < LEVELS - 1:
                c = C[k]
                x = [OUT[t, k, rr, :] + c * x[t] for t in range(2)]
            for t in range(2):
                OUT[t, k, rr, :] = jnp.where(sea, x[t], T[t, k, pl.ds(r + PAD, R), :])
        pltpu.make_async_copy(OUT.at[:, :, rr, :], out_hbm.at[:, :, rr, :], out_sem.at[b]).start()
        return carry

    lax.fori_loop(0, blocks, block, 0)

    def drain(b, carry):
        rr = pl.ds(pl.multiple_of(b * R, R), R)
        pltpu.make_async_copy(OUT.at[:, :, rr, :], out_hbm.at[:, :, rr, :], out_sem.at[b]).wait()
        return carry

    lax.fori_loop(0, blocks, drain, 0)


def column_step(tracers, ec, nc, df, land, surf, pe, pw, south, north, ncs):
    any_ = pl.BlockSpec(memory_space=pl.ANY)
    vm = pl.BlockSpec(memory_space=pltpu.VMEM)
    blocks = 128 // R
    f = jnp.float32
    return pl.pallas_call(
        column_kernel,
        out_shape=jax.ShapeDtypeStruct(tracers.shape, f),
        in_specs=[any_] * 4 + [vm] * 8,
        out_specs=any_,
        scratch_shapes=[
            pltpu.VMEM((2, LEVELS, 144, 128), f),
            pltpu.VMEM((LEVELS, 128, 128), f),
            pltpu.VMEM((LEVELS, 128, 128), f),
            pltpu.VMEM((LEVELS, 128, 128), f),
            pltpu.VMEM((LEVELS, R, 128), f),
            pltpu.VMEM((2, LEVELS, 128, 128), f),
            pltpu.VMEM((2, 2, 2, 128, 128), jnp.bfloat16),
            pltpu.VMEM((2 * G * R, 512), jnp.bfloat16),
            pltpu.VMEM((2 * G * R, 256), f),
            pltpu.VMEM((2, LEVELS, 136, 128), f),
            pltpu.SemaphoreType.DMA((blocks, 4)),
            pltpu.SemaphoreType.DMA((blocks,)),
        ],
        compiler_params=pltpu.CompilerParams(vmem_limit_bytes=52 << 20),
        name="column_step",
    )(tracers, ec, nc, df, stencil_weights(), land, surf, pe, pw, south, north, ncs)
FIELDS = 5
CAP_ROWS = 48
SRC0 = 80
WGT0 = 128
LINK_ROWS = 176
MESH = pl.DeviceIdType.MESH


def exchange_kernel(tr_hbm, ec_hbm, nc_hbm, flux_ref, src_ref, wgt_ref, tgt_ref,
                    surf_ref, pe_ref, pw_ref, south_ref, north_ref, ncs_ref,
                    T, EC, NC, L, RL, TG, WP, Z, B, Q, pe_out, pw_out, rows_out, nc_out, load_sem, send_sem, recv_sem):
    rows, cols = 128, 128
    lat, lon = lax.axis_index("lat"), lax.axis_index("lon")
    nlat, nlon = lax.axis_size("lat"), lax.axis_size("lon")
    north, south = lax.rem(lat + 1, nlat), lax.rem(lat + nlat - 1, nlat)
    east, west = lax.rem(lon + 1, nlon), lax.rem(lon + nlon - 1, nlon)

    loads = [
        pltpu.make_async_copy(tr_hbm, T, load_sem.at[0]),
        pltpu.make_async_copy(ec_hbm, EC, load_sem.at[1]),
        pltpu.make_async_copy(nc_hbm.at[:, rows - 8:rows, :], NC, load_sem.at[2]),
    ]
    for c in loads:
        c.start()

    barrier = pltpu.get_barrier_semaphore()
    for peer in ((lat, east), (lat, west), (north, lon), (south, lon), (north, east), (south, west)):
        pl.semaphore_signal(barrier, inc=1, device_id=peer, device_id_type=MESH)

    field = lax.broadcasted_iota(jnp.int32, (8, cols), 0)
    for n in range(4):
        for h in range(16):
            lanes = pl.ds(n * 2048 + h * 128, 128)
            tile = flux_ref[0:6, lanes]
            more = jnp.where(field[0:5] == 1, jnp.broadcast_to(tile[5:6], (5, cols)), 0.0)
            L[n, h * FIELDS:(h + 1) * FIELDS, :] = tile[0:5] + more
        for j in range(CAP_ROWS):
            lanes = pl.ds(j * 128, 128)
            L[n, SRC0 + j:SRC0 + j + 1, :] = (src_ref[0, n:n + 1, lanes] - n * 2048).astype(jnp.float32)
            L[n, WGT0 + j:WGT0 + j + 1, :] = wgt_ref[0, n:n + 1, lanes]
            TG[n, j:j + 1, :] = tgt_ref[0, n:n + 1, lanes]

    pl.semaphore_wait(barrier, 6)

    def send(src, dst, at, peer):
        copy = pltpu.make_async_remote_copy(
            src_ref=src, dst_ref=dst, send_sem=send_sem.at[at], recv_sem=recv_sem.at[at],
            device_id=peer, device_id_type=MESH)
        copy.start()
        return copy

    links = {
        1: send(L.at[1], RL.at[0], 0, (lat, east)),
        2: send(L.at[2], RL.at[1], 1, (north, lon)),
        3: send(L.at[3], RL.at[2], 2, (north, east)),
    }

    sub16 = lax.broadcasted_iota(jnp.int32, (16, cols), 0).astype(jnp.float32)

    def remap(n, box):
        exists = jnp.where(lat >= n // 2, 1.0, 0.0)

        def pick(g, carry):
            at = pl.ds(pl.multiple_of(g * 8, 8), 8)
            cell = box[pl.ds(pl.multiple_of(SRC0 + g * 8, 8), 8), :].astype(jnp.int32)
            weight = box[pl.ds(pl.multiple_of(WGT0 + g * 8, 8), 8), :] * exists
            low = cell & 127
            high = cell >> 7
            for f in range(FIELDS):
                got = jnp.zeros((8, cols), jnp.float32)
                for h in range(16):
                    row = jnp.broadcast_to(box[h * FIELDS + f:h * FIELDS + f + 1, :], (8, cols))
                    got = jnp.where(high == h, jnp.take_along_axis(row, low, axis=1), got)
                got = got * weight
                top = got.astype(jnp.bfloat16).astype(jnp.float32)
                WP[f, at, :] = top
                WP[FIELDS + f, at, :] = got - top
            return carry

        lax.fori_loop(0, CAP_ROWS // 8, pick, 0)

        def hot(q, carry):
            for u in range(4):
                j = q * 4 + u
                lanes = pl.ds(pl.multiple_of(j * 128, 128), 128)
                cell = TG[n, pl.ds(j, 1), :]
                row = (cell >> 7) & 63
                col = cell & 63
                a = jnp.broadcast_to((row >> 2).astype(jnp.float32), (16, cols)) == sub16
                b = jnp.broadcast_to((((row & 3) << 6) + col).astype(jnp.float32), (16, cols))
                for w in range(2 * FIELDS):
                    v = jnp.broadcast_to(WP[w, pl.ds(j, 1), :], (16, cols))
                    Z[w * 16:(w + 1) * 16, lanes] = jnp.where(a, v, 0.0).astype(jnp.bfloat16)
                for s in range(16):
                    B[s * 16:(s + 1) * 16, lanes] = jnp.where(b == sub16 + 16.0 * s, 1.0, 0.0).astype(jnp.bfloat16)
            return carry

        lax.fori_loop(0, CAP_ROWS // 4, hot, 0)
        quad = lax.dot_general(Z[...], B[...], (((1,), (1,)), ((), ())), preferred_element_type=jnp.float32)
        col0 = (1 - n % 2) * 64
        for f in range(FIELDS):
            total = quad[f * 16:(f + 1) * 16] + quad[(FIELDS + f) * 16:(FIELDS + f + 1) * 16]
            for i in range(4):
                part = total[:, (i // 2) * 128:(i // 2 + 1) * 128]
                if (i % 2) * 64 != col0:
                    part = pltpu.roll(part, 64, 1)
                Q[n, f, i] = part

    remap(0, L.at[0])

    for c in loads:
        c.wait()
    lane = lax.broadcasted_iota(jnp.int32, (64, cols), 1)
    for t in range(2):
        for z in range(2):
            rr = pl.ds(z * 64, 64)

            def pack(q, carry):
                pe, pw = carry
                for u in range(8):
                    k = q * 8 + u
                    half = k // HALF
                    j = k - half * HALF
                    by = 4 * j + 2 * (1 - half)
                    y = pltpu.roll(T[t, k, rr, :], by, 1)
                    off = (lane - by) & 127
                    pe = jnp.where(off < 2, y, pe)
                    pw = jnp.where(off >= 126, y, pw)
                return pe, pw

            zero = jnp.zeros((64, cols), jnp.float32)
            pe, pw = lax.fori_loop(0, LEVELS // 8, pack, (zero, zero))

            def pack_courant(q, pw):
                for u in range(8):
                    j = q * 8 + u
                    y = pltpu.roll(EC[t * HALF + j, rr, :], j + 97, 1)
                    pw = jnp.where(lane == 96 + j, y, pw)
                return pw

            pw = lax.fori_loop(0, HALF // 8, pack_courant, pw)
            pe_out[t, rr, :] = pe
            pw_out[t, rr, :] = pw

    def edge_rows(k, carry):
        for t in range(2):
            rows_out[0, t, k] = T[t, k, 0:2, :]
            rows_out[1, t, k] = T[t, k, rows - 2:rows, :]
        nc_out[k] = NC[k, 7:8, :]
        return carry

    lax.fori_loop(0, LEVELS, edge_rows, 0)

    halos = [
        send(pe_out, pe_ref, 3, (lat, west)),
        send(pw_out, pw_ref, 4, (lat, east)),
        send(rows_out.at[0], north_ref, 5, (south, lon)),
        send(rows_out.at[1], south_ref, 6, (north, lon)),
        send(nc_out, ncs_ref, 7, (north, lon)),
    ]

    for n in (2, 1, 3):
        links[n].wait()
        remap(n, RL.at[n - 1])

    left = lax.broadcasted_iota(jnp.int32, (16, cols), 1) < 64
    for a in range(2):
        for f in range(FIELDS):
            for i in range(4):
                surf_ref[f, pl.ds((1 - a) * 64 + i, 16, stride=4), :] = jnp.where(left, Q[2 * a + 1, f, i], Q[2 * a, f, i])

    for c in halos:
        c.wait()
    below = jnp.where(lat > 0, 1.0, 0.0)
    over = jnp.where(lat < nlat - 1, 1.0, 0.0)
    south_ref[...] = south_ref[...] * below
    ncs_ref[...] = ncs_ref[...] * below
    north_ref[...] = north_ref[...] * over


def exchange(tracers, ec, nc, fluxes, source_cell, link_weight, target_cell):
    any_ = pl.BlockSpec(memory_space=pl.ANY)
    vm = pl.BlockSpec(memory_space=pltpu.VMEM)
    f = jnp.float32
    s = jax.ShapeDtypeStruct
    return pl.pallas_call(
        exchange_kernel,
        out_shape=[s((FIELDS, 128, 128), f), s((2, 128, 128), f), s((2, 128, 128), f), s((2, LEVELS, 2, 128), f),
                   s((2, LEVELS, 2, 128), f), s((LEVELS, 1, 128), f)],
        in_specs=[any_] * 3 + [vm] * 4,
        out_specs=[vm] * 6,
        scratch_shapes=[
            pltpu.VMEM((2, LEVELS, 128, 128), f),
            pltpu.VMEM((LEVELS, 128, 128), f),
            pltpu.VMEM((LEVELS, 8, 128), f),
            pltpu.VMEM((4, LINK_ROWS, 128), f),
            pltpu.VMEM((3, LINK_ROWS, 128), f),
            pltpu.VMEM((4, CAP_ROWS, 128), jnp.int32),
            pltpu.VMEM((2 * FIELDS, CAP_ROWS, 128), f),
            pltpu.VMEM((2 * FIELDS * 16, 6144), jnp.bfloat16),
            pltpu.VMEM((256, 6144), jnp.bfloat16),
            pltpu.VMEM((4, FIELDS, 4, 16, 128), f),
            pltpu.VMEM((2, 128, 128), f),
            pltpu.VMEM((2, 128, 128), f),
            pltpu.VMEM((2, 2, LEVELS, 2, 128), f),
            pltpu.VMEM((LEVELS, 1, 128), f),
            pltpu.SemaphoreType.DMA((3,)),
            pltpu.SemaphoreType.DMA((8,)),
            pltpu.SemaphoreType.DMA((8,)),
        ],
        compiler_params=pltpu.CompilerParams(collective_id=0, has_side_effects=True, vmem_limit_bytes=40 << 20),
        name="exchange",
    )(tracers, ec, nc, fluxes, source_cell, link_weight, target_cell)


def local(tracers, east_courant, north_courant, diffusivity, land_sea, fluxes, source_cell, link_weight, target_cell):
    surf, pe, pw, south, north, ncs = exchange(
        tracers, east_courant, north_courant, fluxes, source_cell, link_weight, target_cell)
    return column_step(tracers, east_courant, north_courant, diffusivity, land_sea, surf, pe, pw, south, north, ncs)


def solution(mesh):
    in_specs = (
        P(None, None, "lat", "lon"),
        P(None, "lat", "lon"),
        P(None, "lat", "lon"),
        P(None, "lat", "lon"),
        P("lat", "lon"),
        P(None, ("lat", "lon")),
        P(("lat", "lon"), None, None),
        P(("lat", "lon"), None, None),
        P(("lat", "lon"), None, None),
    )
    out_specs = P(None, None, "lat", "lon")
    return jax.shard_map(local, mesh=mesh, in_specs=in_specs, out_specs=out_specs, check_vma=False)
```

```python
import math
import jax, jax.numpy as jnp
import numpy as np
from jax import lax
from jax.experimental import pallas as pl
from jax.experimental.pallas import tpu as pltpu
from jax.sharding import PartitionSpec as P

LEVELS = 48
HALF = 24
R = 32
G = 8
PAD = 8


def stencil_weights():
    cols = 128
    main = np.zeros((cols, 2 * cols), np.float32)
    for i in range(cols):
        for off, w in ((-1, -1), (0, 7), (1, 7), (2, -1)):
            if 0 <= i + off < cols:
                main[i + off, i] = w
        for off, w in ((-2, -1), (-1, 7), (0, 7), (1, -1)):
            if 0 <= i + off < cols:
                main[i + off, cols + i] = w
    halves = []
    for half in range(2):
        edge = np.zeros((cols, 2 * cols), np.float32)
        order = (-2, -1, 128, 129) if half == 0 else (128, 129, -2, -1)
        for lane in range(cols):
            p = order[lane % 4]
            for i in range(cols):
                edge[lane, i] = {-1: -1, 0: 7, 1: 7, 2: -1}.get(p - i, 0)
                edge[lane, cols + i] = {-2: -1, -1: 7, 0: 7, 1: -1}.get(p - i, 0)
        halves.append(np.concatenate([main, main, edge, edge], 0))
    return jnp.asarray(np.stack(halves), jnp.bfloat16)


def two_pieces(x):
    high = x.astype(jnp.bfloat16)
    return high, (x - high.astype(jnp.float32)).astype(jnp.bfloat16)


def column_kernel(tr_hbm, ec_hbm, nc_hbm, df_hbm, w_ref, land_ref, surf_ref, pe_ref, pw_ref, south_ref, north_ref, ncs_ref,
                  out_hbm, T, EC, NC, DF, C, OUT, H, X, S, FN, tr_sem, co_sem, df_sem, out_sem):
    rows, cols = 128, 128
    blocks = rows // R

    groups = LEVELS // G

    def span(i, size):
        return pl.ds(pl.multiple_of(i * size, size), size)

    def load_tracers(b, g):
        return pltpu.make_async_copy(
            tr_hbm.at[:, span(g, G), span(b, R), :],
            T.at[:, span(g, G), pl.ds(pl.multiple_of(b * R + PAD, PAD), R), :], tr_sem.at[b, g])

    def load_courants(b, g):
        return [pltpu.make_async_copy(h.at[span(g, G), span(b, R), :], v.at[span(g, G), span(b, R), :], co_sem.at[p, b, g])
                for p, (h, v) in enumerate(((ec_hbm, EC), (nc_hbm, NC)))]

    def load_diffusivity(b):
        return pltpu.make_async_copy(df_hbm.at[:, span(b, R), :], DF.at[:, span(b, R), :], df_sem.at[b])

    def start_first(g, carry):
        load_tracers(0, g).start()
        load_tracers(1, g).start()
        for c in load_courants(0, g):
            c.start()
        return carry

    lax.fori_loop(0, groups, start_first, 0)
    load_diffusivity(0).start()

    lane = lax.broadcasted_iota(jnp.int32, (rows, cols), 1)
    low = lane % 4 < 2
    for t in range(2):
        pe, pw = pe_ref[t], pw_ref[t]
        for half in range(2):
            h = jnp.where(low, pw, pe) if half == 0 else jnp.where(low, pe, pw)
            H[t, half, 0], H[t, half, 1] = two_pieces(h)

    def pad_rows(k, carry):
        for t in range(2):
            T[t, k, PAD - 2:PAD, :] = south_ref[t, k]
            T[t, k, PAD + rows:PAD + rows + 2, :] = north_ref[t, k]
        return carry

    lax.fori_loop(0, LEVELS, pad_rows, 0)

    def block(b, carry):
        @pl.when((b > 0) & (b + 1 < blocks))
        def _():
            def start_next(g, carry):
                load_tracers(b + 1, g).start()
                return carry

            lax.fori_loop(0, groups, start_next, 0)

        @pl.when(b + 1 < blocks)
        def _():
            def start_next(g, carry):
                for c in load_courants(b + 1, g):
                    c.start()
                return carry

            lax.fori_loop(0, groups, start_next, 0)
            load_diffusivity(b + 1).start()

        r = pl.multiple_of(b * R, R)
        rr = pl.ds(r, R)
        lane = lax.broadcasted_iota(jnp.int32, (R, cols), 1)
        first = lane == 0
        stress = 2.0 * jnp.sqrt(surf_ref[3, rr, :] * surf_ref[3, rr, :] + surf_ref[4, rr, :] * surf_ref[4, rr, :])

        for half in range(2):
            def group(q, carry):
                g = half * (HALF // G) + q

                @pl.when(b == 0)
                def _():
                    load_tracers(0, g).wait()

                @pl.when(b + 1 < blocks)
                def _():
                    load_tracers(b + 1, g).wait()

                for c in load_courants(b, g):
                    c.wait()

                @pl.when(b == 0)
                def _():
                    for u in range(G):
                        k = g * G + u
                        for t in range(2):
                            s = T[t, k, PAD - 2:PAD - 1, :] + T[t, k, PAD + 1:PAD + 2, :]
                            m = T[t, k, PAD - 1:PAD, :] + T[t, k, PAD:PAD + 1, :]
                            FN[t, k, PAD - 1:PAD, :] = ncs_ref[k] * (7.0 * m - s)

                for u in range(G):
                    j = q * G + u
                    k = half * HALF + j
                    here = (lane + 2 * half) % cols // 4 == j
                    for t in range(2):
                        x = T[t, k, pl.ds(r + PAD, R), :]
                        at = pl.ds((u * 2 + t) * R, R)
                        X[at, 0:cols], X[at, cols:2 * cols] = two_pieces(x)
                        for p in range(2):
                            h = H[t, half, p, rr, :]
                            X[at, (2 + p) * cols:(3 + p) * cols] = jnp.where(here, h, jnp.zeros_like(h))
                S[...] = jnp.dot(X[...], w_ref[half], preferred_element_type=jnp.float32)
                for u in range(G):
                    j = q * G + u
                    k = half * HALF + j
                    ce = EC[k, rr, :]
                    cn = NC[k, rr, :]
                    hec = pltpu.roll(pw_ref[half, rr, :], cols - 96 - j, 1)
                    cw = jnp.where(first, hec, pltpu.roll(ce, 1, 1))
                    for t in range(2):
                        at = pl.ds((u * 2 + t) * R, R)
                        x = T[t, k, pl.ds(r + PAD, R), :]
                        n1 = T[t, k, pl.ds(r + PAD + 1, R), :]
                        n2 = T[t, k, pl.ds(r + PAD + 2, R), :]
                        s1 = T[t, k, pl.ds(r + PAD - 1, R), :]
                        fn = cn * (7.0 * (x + n1) - (s1 + n2))
                        FN[t, k, pl.ds(r + PAD, R), :] = fn
                        fs = FN[t, k, pl.ds(r + PAD - 1, R), :]
                        div = (ce * S[at, 0:cols] - cw * S[at, cols:2 * cols]) + (fn - fs)
                        OUT[t, k, rr, :] = x - div * (1.0 / 12.0)
                return carry

            lax.fori_loop(0, HALF // G, group, 0)

        load_diffusivity(b).wait()
        heat = 0.5 * surf_ref[2, rr, :]
        tops = [0.5 * surf_ref[0, rr, :], 0.5 * surf_ref[1, rr, :]]
        above = None
        cprev = None
        vprev = [None, None]
        for k in range(LEVELS):
            if k < LEVELS - 1:
                below = DF[k, rr, :] + stress * math.exp(-4.0 * k / LEVELS)
            absorb = math.exp(-4.0 * k / LEVELS) - math.exp(-4.0 * (k + 1) / LEVELS)
            adv = [OUT[0, k, rr, :] + heat * absorb, OUT[1, k, rr, :]]
            if k == 0:
                adv[0] = adv[0] + tops[0]
                adv[1] = adv[1] + tops[1]
                inv = 1.0 / (1.0 + below)
                v = [adv[0] * inv, adv[1] * inv]
            else:
                pivot = 1.0 + above * (1.0 - cprev)
                if k < LEVELS - 1:
                    pivot = pivot + below
                inv = 1.0 / pivot
                v = [(adv[t] + above * vprev[t]) * inv for t in range(2)]
            if k < LEVELS - 1:
                cprev = below * inv
                C[k] = cprev
                above = below
                for t in range(2):
                    OUT[t, k, rr, :] = v[t]
            vprev = v
        sea = land_ref[rr, :] == 1
        x = vprev
        for k in range(LEVELS - 1, -1, -1):
            if k < LEVELS - 1:
                c = C[k]
                x = [OUT[t, k, rr, :] + c * x[t] for t in range(2)]
            for t in range(2):
                OUT[t, k, rr, :] = jnp.where(sea, x[t], T[t, k, pl.ds(r + PAD, R), :])
        pltpu.make_async_copy(OUT.at[:, :, rr, :], out_hbm.at[:, :, rr, :], out_sem.at[b]).start()
        return carry

    lax.fori_loop(0, blocks, block, 0)

    def drain(b, carry):
        rr = pl.ds(pl.multiple_of(b * R, R), R)
        pltpu.make_async_copy(OUT.at[:, :, rr, :], out_hbm.at[:, :, rr, :], out_sem.at[b]).wait()
        return carry

    lax.fori_loop(0, blocks, drain, 0)


def column_step(tracers, ec, nc, df, land, surf, pe, pw, south, north, ncs):
    any_ = pl.BlockSpec(memory_space=pltpu.HBM)
    vm = pl.BlockSpec(memory_space=pltpu.VMEM)
    blocks = 128 // R
    f = jnp.float32
    return pl.pallas_call(
        column_kernel,
        out_shape=jax.ShapeDtypeStruct(tracers.shape, f),
        in_specs=[any_] * 4 + [vm] * 8,
        out_specs=any_,
        scratch_shapes=[
            pltpu.VMEM((2, LEVELS, 144, 128), f),
            pltpu.VMEM((LEVELS, 128, 128), f),
            pltpu.VMEM((LEVELS, 128, 128), f),
            pltpu.VMEM((LEVELS, 128, 128), f),
            pltpu.VMEM((LEVELS, R, 128), f),
            pltpu.VMEM((2, LEVELS, 128, 128), f),
            pltpu.VMEM((2, 2, 2, 128, 128), jnp.bfloat16),
            pltpu.VMEM((2 * G * R, 512), jnp.bfloat16),
            pltpu.VMEM((2 * G * R, 256), f),
            pltpu.VMEM((2, LEVELS, 136, 128), f),
            pltpu.SemaphoreType.DMA((blocks, LEVELS // G)),
            pltpu.SemaphoreType.DMA((2, blocks, LEVELS // G)),
            pltpu.SemaphoreType.DMA((blocks,)),
            pltpu.SemaphoreType.DMA((blocks,)),
        ],
        compiler_params=pltpu.CompilerParams(vmem_limit_bytes=60 << 20),
        name="column_step",
    )(tracers, ec, nc, df, stencil_weights(), land, surf, pe, pw, south, north, ncs)
FIELDS = 5
CAP_ROWS = 48
SRC0 = 80
WGT0 = 128
LINK_ROWS = 176
MESH = pl.DeviceIdType.MESH


def exchange_kernel(tr_hbm, ec_hbm, nc_hbm, flux_hbm, src_hbm, wgt_hbm, tgt_hbm,
                    surf_ref, pe_ref, pw_ref, south_ref, north_ref, ncs_ref,
                    T, EC, NC, flux_ref, src_ref, wgt_ref, tgt_ref,
                    L, RL, TG, WP, Z, B, Q, pe_out, pw_out, rows_out, nc_out, load_sem, send_sem, recv_sem):
    rows, cols = 128, 128
    lat, lon = lax.axis_index("lat"), lax.axis_index("lon")
    nlat, nlon = lax.axis_size("lat"), lax.axis_size("lon")
    north, south = lax.rem(lat + 1, nlat), lax.rem(lat + nlat - 1, nlat)
    east, west = lax.rem(lon + 1, nlon), lax.rem(lon + nlon - 1, nlon)

    loads = [
        pltpu.make_async_copy(src_hbm, src_ref, load_sem.at[0]),
        pltpu.make_async_copy(wgt_hbm, wgt_ref, load_sem.at[1]),
        pltpu.make_async_copy(flux_hbm, flux_ref, load_sem.at[2]),
        pltpu.make_async_copy(tgt_hbm, tgt_ref, load_sem.at[3]),
        pltpu.make_async_copy(tr_hbm, T, load_sem.at[4]),
        pltpu.make_async_copy(ec_hbm, EC, load_sem.at[5]),
        pltpu.make_async_copy(nc_hbm.at[:, rows - 8:rows, :], NC, load_sem.at[6]),
    ]
    for c in loads:
        c.start()

    barrier = pltpu.get_barrier_semaphore()
    for peer in ((lat, east), (lat, west), (north, lon), (south, lon), (north, east), (south, west)):
        pl.semaphore_signal(barrier, inc=1, device_id=peer, device_id_type=MESH)

    for c in loads[:4]:
        c.wait()
    field = lax.broadcasted_iota(jnp.int32, (8, cols), 0)
    for n in range(4):
        for h in range(16):
            lanes = pl.ds(n * 2048 + h * 128, 128)
            tile = flux_ref[0:6, lanes]
            more = jnp.where(field[0:5] == 1, jnp.broadcast_to(tile[5:6], (5, cols)), 0.0)
            L[n, h * FIELDS:(h + 1) * FIELDS, :] = tile[0:5] + more
        for j in range(CAP_ROWS):
            lanes = pl.ds(j * 128, 128)
            L[n, SRC0 + j:SRC0 + j + 1, :] = (src_ref[0, n:n + 1, lanes] - n * 2048).astype(jnp.float32)
            L[n, WGT0 + j:WGT0 + j + 1, :] = wgt_ref[0, n:n + 1, lanes]
            TG[n, j:j + 1, :] = tgt_ref[0, n:n + 1, lanes]

    pl.semaphore_wait(barrier, 6)

    def send(src, dst, at, peer):
        copy = pltpu.make_async_remote_copy(
            src_ref=src, dst_ref=dst, send_sem=send_sem.at[at], recv_sem=recv_sem.at[at],
            device_id=peer, device_id_type=MESH)
        copy.start()
        return copy

    links = {
        1: send(L.at[1], RL.at[0], 0, (lat, east)),
        2: send(L.at[2], RL.at[1], 1, (north, lon)),
        3: send(L.at[3], RL.at[2], 2, (north, east)),
    }

    b16 = jnp.bfloat16
    sub16 = lax.broadcasted_iota(jnp.int32, (16, cols), 0).astype(jnp.float32)
    subs = [(sub16 + 16.0 * s).astype(b16) for s in range(16)]
    one, zero16 = jnp.ones((16, cols), b16), jnp.zeros((16, cols), b16)

    def remap(n, box):
        exists = jnp.where(lat >= n // 2, 1.0, 0.0)

        def pick(g, carry):
            at = pl.ds(pl.multiple_of(g * 8, 8), 8)
            cell = box[pl.ds(pl.multiple_of(SRC0 + g * 8, 8), 8), :].astype(jnp.int32)
            weight = box[pl.ds(pl.multiple_of(WGT0 + g * 8, 8), 8), :] * exists
            low = cell & 127
            high = cell >> 7
            for f in range(FIELDS):
                got = jnp.zeros((8, cols), jnp.float32)
                for h in range(16):
                    row = jnp.broadcast_to(box[h * FIELDS + f:h * FIELDS + f + 1, :], (8, cols))
                    got = jnp.where(high == h, jnp.take_along_axis(row, low, axis=1), got)
                got = got * weight
                top = got.astype(jnp.bfloat16).astype(jnp.float32)
                WP[f, at, :] = top
                WP[FIELDS + f, at, :] = got - top
            return carry

        lax.fori_loop(0, CAP_ROWS // 8, pick, 0)

        def hot(q, carry):
            for u in range(4):
                j = q * 4 + u
                lanes = pl.ds(pl.multiple_of(j * 128, 128), 128)
                cell = TG[n, pl.ds(j, 1), :]
                row = (cell >> 7) & 63
                col = cell & 63
                a = jnp.broadcast_to((row >> 2).astype(jnp.float32), (16, cols)).astype(b16) == subs[0]
                b = jnp.broadcast_to((((row & 3) << 6) + col).astype(jnp.float32), (16, cols)).astype(b16)
                for w in range(2 * FIELDS):
                    v = jnp.broadcast_to(WP[w, pl.ds(j, 1), :], (16, cols)).astype(b16)
                    Z[w * 16:(w + 1) * 16, lanes] = jnp.where(a, v, zero16)
                for s in range(16):
                    B[s * 16:(s + 1) * 16, lanes] = jnp.where(b == subs[s], one, zero16)
            return carry

        lax.fori_loop(0, CAP_ROWS // 4, hot, 0)
        quad = lax.dot_general(Z[...], B[...], (((1,), (1,)), ((), ())), preferred_element_type=jnp.float32)
        col0 = (1 - n % 2) * 64
        for f in range(FIELDS):
            total = quad[f * 16:(f + 1) * 16] + quad[(FIELDS + f) * 16:(FIELDS + f + 1) * 16]
            for i in range(4):
                part = total[:, (i // 2) * 128:(i // 2 + 1) * 128]
                if (i % 2) * 64 != col0:
                    part = pltpu.roll(part, 64, 1)
                Q[n, f, i] = part

    remap(0, L.at[0])

    for c in loads[4:]:
        c.wait()
    lane = lax.broadcasted_iota(jnp.int32, (64, cols), 1)
    for t in range(2):
        for z in range(2):
            rr = pl.ds(z * 64, 64)

            def pack(q, carry):
                pe, pw = carry
                for u in range(8):
                    k = q * 8 + u
                    half = k // HALF
                    j = k - half * HALF
                    by = 4 * j + 2 * (1 - half)
                    y = pltpu.roll(T[t, k, rr, :], by, 1)
                    off = (lane - by) & 127
                    pe = jnp.where(off < 2, y, pe)
                    pw = jnp.where(off >= 126, y, pw)
                return pe, pw

            zero = jnp.zeros((64, cols), jnp.float32)
            pe, pw = lax.fori_loop(0, LEVELS // 8, pack, (zero, zero))

            def pack_courant(q, pw):
                for u in range(8):
                    j = q * 8 + u
                    y = pltpu.roll(EC[t * HALF + j, rr, :], j + 97, 1)
                    pw = jnp.where(lane == 96 + j, y, pw)
                return pw

            pw = lax.fori_loop(0, HALF // 8, pack_courant, pw)
            pe_out[t, rr, :] = pe
            pw_out[t, rr, :] = pw

    def edge_rows(k, carry):
        for t in range(2):
            rows_out[0, t, k] = T[t, k, 0:2, :]
            rows_out[1, t, k] = T[t, k, rows - 2:rows, :]
        nc_out[k] = NC[k, 7:8, :]
        return carry

    lax.fori_loop(0, LEVELS, edge_rows, 0)

    halos = [
        send(pe_out, pe_ref, 3, (lat, west)),
        send(pw_out, pw_ref, 4, (lat, east)),
        send(rows_out.at[0], north_ref, 5, (south, lon)),
        send(rows_out.at[1], south_ref, 6, (north, lon)),
        send(nc_out, ncs_ref, 7, (north, lon)),
    ]

    for n in (2, 1, 3):
        links[n].wait()
        remap(n, RL.at[n - 1])

    left = lax.broadcasted_iota(jnp.int32, (16, cols), 1) < 64
    for a in range(2):
        for f in range(FIELDS):
            for i in range(4):
                surf_ref[f, pl.ds((1 - a) * 64 + i, 16, stride=4), :] = jnp.where(left, Q[2 * a + 1, f, i], Q[2 * a, f, i])

    for c in halos:
        c.wait()
    below = jnp.where(lat > 0, 1.0, 0.0)
    over = jnp.where(lat < nlat - 1, 1.0, 0.0)
    south_ref[...] = south_ref[...] * below
    ncs_ref[...] = ncs_ref[...] * below
    north_ref[...] = north_ref[...] * over


def exchange(tracers, ec, nc, fluxes, source_cell, link_weight, target_cell):
    hbm = pl.BlockSpec(memory_space=pltpu.HBM)
    vm = pl.BlockSpec(memory_space=pltpu.VMEM)
    f = jnp.float32
    s = jax.ShapeDtypeStruct
    return pl.pallas_call(
        exchange_kernel,
        out_shape=[s((FIELDS, 128, 128), f), s((2, 128, 128), f), s((2, 128, 128), f), s((2, LEVELS, 2, 128), f),
                   s((2, LEVELS, 2, 128), f), s((LEVELS, 1, 128), f)],
        in_specs=[hbm] * 7,
        out_specs=[vm] * 6,
        scratch_shapes=[
            pltpu.VMEM((2, LEVELS, 128, 128), f),
            pltpu.VMEM((LEVELS, 128, 128), f),
            pltpu.VMEM((LEVELS, 8, 128), f),
            pltpu.VMEM((6, 8192), f),
            pltpu.VMEM((1, 4, 6144), jnp.int32),
            pltpu.VMEM((1, 4, 6144), f),
            pltpu.VMEM((1, 4, 6144), jnp.int32),
            pltpu.VMEM((4, LINK_ROWS, 128), f),
            pltpu.VMEM((3, LINK_ROWS, 128), f),
            pltpu.VMEM((4, CAP_ROWS, 128), jnp.int32),
            pltpu.VMEM((2 * FIELDS, CAP_ROWS, 128), f),
            pltpu.VMEM((2 * FIELDS * 16, 6144), jnp.bfloat16),
            pltpu.VMEM((256, 6144), jnp.bfloat16),
            pltpu.VMEM((4, FIELDS, 4, 16, 128), f),
            pltpu.VMEM((2, 128, 128), f),
            pltpu.VMEM((2, 128, 128), f),
            pltpu.VMEM((2, 2, LEVELS, 2, 128), f),
            pltpu.VMEM((LEVELS, 1, 128), f),
            pltpu.SemaphoreType.DMA((7,)),
            pltpu.SemaphoreType.DMA((8,)),
            pltpu.SemaphoreType.DMA((8,)),
        ],
        compiler_params=pltpu.CompilerParams(collective_id=0, has_side_effects=True, vmem_limit_bytes=60 << 20),
        name="exchange",
    )(tracers, ec, nc, fluxes, source_cell, link_weight, target_cell)


def local(tracers, east_courant, north_courant, diffusivity, land_sea, fluxes, source_cell, link_weight, target_cell):
    surf, pe, pw, south, north, ncs = exchange(
        tracers, east_courant, north_courant, fluxes, source_cell, link_weight, target_cell)
    return column_step(tracers, east_courant, north_courant, diffusivity, land_sea, surf, pe, pw, south, north, ncs)


def solution(mesh):
    in_specs = (
        P(None, None, "lat", "lon"),
        P(None, "lat", "lon"),
        P(None, "lat", "lon"),
        P(None, "lat", "lon"),
        P("lat", "lon"),
        P(None, ("lat", "lon")),
        P(("lat", "lon"), None, None),
        P(("lat", "lon"), None, None),
        P(("lat", "lon"), None, None),
    )
    out_specs = P(None, None, "lat", "lon")
    return jax.shard_map(local, mesh=mesh, in_specs=in_specs, out_specs=out_specs, check_vma=False)
```

```python
import math
import jax, jax.numpy as jnp
import numpy as np
from jax import lax
from jax.experimental import pallas as pl
from jax.experimental.pallas import tpu as pltpu
from jax.sharding import PartitionSpec as P

LEVELS = 48
HALF = 24
R = 32
G = 12
PAD = 8


def stencil_weights():
    cols = 128
    main = np.zeros((cols, 2 * cols), np.float32)
    for i in range(cols):
        for off, w in ((-1, -1), (0, 7), (1, 7), (2, -1)):
            if 0 <= i + off < cols:
                main[i + off, i] = w
        for off, w in ((-2, -1), (-1, 7), (0, 7), (1, -1)):
            if 0 <= i + off < cols:
                main[i + off, cols + i] = w
    halves = []
    for half in range(2):
        edge = np.zeros((cols, 2 * cols), np.float32)
        order = (-2, -1, 128, 129) if half == 0 else (128, 129, -2, -1)
        for lane in range(cols):
            p = order[lane % 4]
            for i in range(cols):
                edge[lane, i] = {-1: -1, 0: 7, 1: 7, 2: -1}.get(p - i, 0)
                edge[lane, cols + i] = {-2: -1, -1: 7, 0: 7, 1: -1}.get(p - i, 0)
        halves.append(np.concatenate([main, main, edge, edge], 0))
    return jnp.asarray(np.stack(halves), jnp.bfloat16)


def two_pieces(x):
    high = x.astype(jnp.bfloat16)
    return high, (x - high.astype(jnp.float32)).astype(jnp.bfloat16)


def column_kernel(tr_hbm, ec_hbm, nc_hbm, df_hbm, w_ref, land_ref, surf_ref, pe_ref, pw_ref, south_ref, north_ref, ncs_ref,
                  out_hbm, T, EC, NC, DF, C, OUT, H, X, S, FN, tr_sem, co_sem, df_sem, out_sem):
    rows, cols = 128, 128
    blocks = rows // R

    groups = LEVELS // G

    def span(i, size):
        return pl.ds(pl.multiple_of(i * size, size), size)

    def load_tracers(b, g):
        return pltpu.make_async_copy(
            tr_hbm.at[:, span(g, G), span(b, R), :],
            T.at[:, span(g, G), pl.ds(pl.multiple_of(b * R + PAD, PAD), R), :], tr_sem.at[b, g])

    def load_courants(b, g):
        return [pltpu.make_async_copy(h.at[span(g, G), span(b, R), :], v.at[span(g, G), span(b, R), :], co_sem.at[p, b, g])
                for p, (h, v) in enumerate(((ec_hbm, EC), (nc_hbm, NC)))]

    def load_diffusivity(b):
        return pltpu.make_async_copy(df_hbm.at[:, span(b, R), :], DF.at[:, span(b, R), :], df_sem.at[b])

    def start_block(b, carry):
        def start_group(g, carry):
            @pl.when(b == 0)
            def _():
                load_tracers(0, g).start()

            @pl.when(b + 1 < blocks)
            def _():
                load_tracers(b + 1, g).start()

            for c in load_courants(b, g):
                c.start()
            return carry

        lax.fori_loop(0, groups, start_group, 0)
        load_diffusivity(b).start()
        return carry

    lax.fori_loop(0, blocks, start_block, 0)

    lane = lax.broadcasted_iota(jnp.int32, (rows, cols), 1)
    low = lane % 4 < 2
    for t in range(2):
        pe, pw = pe_ref[t], pw_ref[t]
        for half in range(2):
            h = jnp.where(low, pw, pe) if half == 0 else jnp.where(low, pe, pw)
            H[t, half, 0], H[t, half, 1] = two_pieces(h)

    def pad_rows(k, carry):
        for t in range(2):
            T[t, k, PAD - 2:PAD, :] = south_ref[t, k]
            T[t, k, PAD + rows:PAD + rows + 2, :] = north_ref[t, k]
        return carry

    lax.fori_loop(0, LEVELS, pad_rows, 0)

    def block(b, carry):
        r = pl.multiple_of(b * R, R)
        rr = pl.ds(r, R)
        lane = lax.broadcasted_iota(jnp.int32, (R, cols), 1)
        first = lane == 0
        stress = 2.0 * jnp.sqrt(surf_ref[3, rr, :] * surf_ref[3, rr, :] + surf_ref[4, rr, :] * surf_ref[4, rr, :])

        for half in range(2):
            def group(q, carry):
                g = half * (HALF // G) + q

                @pl.when(b == 0)
                def _():
                    load_tracers(0, g).wait()

                @pl.when(b + 1 < blocks)
                def _():
                    load_tracers(b + 1, g).wait()

                for c in load_courants(b, g):
                    c.wait()

                @pl.when(b == 0)
                def _():
                    for u in range(G):
                        k = g * G + u
                        for t in range(2):
                            s = T[t, k, PAD - 2:PAD - 1, :] + T[t, k, PAD + 1:PAD + 2, :]
                            m = T[t, k, PAD - 1:PAD, :] + T[t, k, PAD:PAD + 1, :]
                            FN[t, k, PAD - 1:PAD, :] = ncs_ref[k] * (7.0 * m - s)

                for u in range(G):
                    j = q * G + u
                    k = half * HALF + j
                    here = ((lane + 2 * half) & (cols - 1)) >> 2 == j
                    for t in range(2):
                        x = T[t, k, pl.ds(r + PAD, R), :]
                        at = pl.ds((u * 2 + t) * R, R)
                        X[at, 0:cols], X[at, cols:2 * cols] = two_pieces(x)
                        for p in range(2):
                            h = H[t, half, p, rr, :]
                            X[at, (2 + p) * cols:(3 + p) * cols] = jnp.where(here, h, jnp.zeros_like(h))
                S[...] = jnp.dot(X[...], w_ref[half], preferred_element_type=jnp.float32)
                for u in range(G):
                    j = q * G + u
                    k = half * HALF + j
                    ce = EC[k, rr, :]
                    cn = NC[k, rr, :]
                    hec = pltpu.roll(pw_ref[half, rr, :], cols - 96 - j, 1)
                    cw = jnp.where(first, hec, pltpu.roll(ce, 1, 1))
                    for t in range(2):
                        at = pl.ds((u * 2 + t) * R, R)
                        x = T[t, k, pl.ds(r + PAD, R), :]
                        n1 = T[t, k, pl.ds(r + PAD + 1, R), :]
                        n2 = T[t, k, pl.ds(r + PAD + 2, R), :]
                        s1 = T[t, k, pl.ds(r + PAD - 1, R), :]
                        fn = cn * (7.0 * (x + n1) - (s1 + n2))
                        FN[t, k, pl.ds(r + PAD, R), :] = fn
                        fs = FN[t, k, pl.ds(r + PAD - 1, R), :]
                        div = (ce * S[at, 0:cols] - cw * S[at, cols:2 * cols]) + (fn - fs)
                        OUT[t, k, rr, :] = x - div * (1.0 / 12.0)
                return carry

            lax.fori_loop(0, HALF // G, group, 0)

        load_diffusivity(b).wait()
        heat = 0.5 * surf_ref[2, rr, :]
        tops = [0.5 * surf_ref[0, rr, :], 0.5 * surf_ref[1, rr, :]]
        above = None
        cprev = None
        vprev = [None, None]
        for k in range(LEVELS):
            if k < LEVELS - 1:
                below = DF[k, rr, :] + stress * math.exp(-4.0 * k / LEVELS)
            absorb = math.exp(-4.0 * k / LEVELS) - math.exp(-4.0 * (k + 1) / LEVELS)
            adv = [OUT[0, k, rr, :] + heat * absorb, OUT[1, k, rr, :]]
            if k == 0:
                adv[0] = adv[0] + tops[0]
                adv[1] = adv[1] + tops[1]
                inv = 1.0 / (1.0 + below)
                v = [adv[0] * inv, adv[1] * inv]
            else:
                pivot = 1.0 + above * (1.0 - cprev)
                if k < LEVELS - 1:
                    pivot = pivot + below
                inv = 1.0 / pivot
                v = [(adv[t] + above * vprev[t]) * inv for t in range(2)]
            if k < LEVELS - 1:
                cprev = below * inv
                C[k] = cprev
                above = below
                for t in range(2):
                    OUT[t, k, rr, :] = v[t]
            vprev = v
        sea = land_ref[rr, :] == 1
        x = vprev
        for k in range(LEVELS - 1, -1, -1):
            if k < LEVELS - 1:
                c = C[k]
                x = [OUT[t, k, rr, :] + c * x[t] for t in range(2)]
            for t in range(2):
                OUT[t, k, rr, :] = jnp.where(sea, x[t], T[t, k, pl.ds(r + PAD, R), :])
        pltpu.make_async_copy(OUT.at[:, :, rr, :], out_hbm.at[:, :, rr, :], out_sem.at[b]).start()
        return carry

    lax.fori_loop(0, blocks, block, 0)

    def drain(b, carry):
        rr = pl.ds(pl.multiple_of(b * R, R), R)
        pltpu.make_async_copy(OUT.at[:, :, rr, :], out_hbm.at[:, :, rr, :], out_sem.at[b]).wait()
        return carry

    lax.fori_loop(0, blocks, drain, 0)


def column_step(tracers, ec, nc, df, land, surf, pe, pw, south, north, ncs):
    any_ = pl.BlockSpec(memory_space=pltpu.HBM)
    vm = pl.BlockSpec(memory_space=pltpu.VMEM)
    blocks = 128 // R
    f = jnp.float32
    return pl.pallas_call(
        column_kernel,
        out_shape=jax.ShapeDtypeStruct(tracers.shape, f),
        in_specs=[any_] * 4 + [vm] * 8,
        out_specs=any_,
        scratch_shapes=[
            pltpu.VMEM((2, LEVELS, 144, 128), f),
            pltpu.VMEM((LEVELS, 128, 128), f),
            pltpu.VMEM((LEVELS, 128, 128), f),
            pltpu.VMEM((LEVELS, 128, 128), f),
            pltpu.VMEM((LEVELS, R, 128), f),
            pltpu.VMEM((2, LEVELS, 128, 128), f),
            pltpu.VMEM((2, 2, 2, 128, 128), jnp.bfloat16),
            pltpu.VMEM((2 * G * R, 512), jnp.bfloat16),
            pltpu.VMEM((2 * G * R, 256), f),
            pltpu.VMEM((2, LEVELS, 136, 128), f),
            pltpu.SemaphoreType.DMA((blocks, LEVELS // G)),
            pltpu.SemaphoreType.DMA((2, blocks, LEVELS // G)),
            pltpu.SemaphoreType.DMA((blocks,)),
            pltpu.SemaphoreType.DMA((blocks,)),
        ],
        compiler_params=pltpu.CompilerParams(vmem_limit_bytes=60 << 20),
        name="column_step",
    )(tracers, ec, nc, df, stencil_weights(), land, surf, pe, pw, south, north, ncs)
FIELDS = 5
CAP_ROWS = 48
SRC0 = 80
WGT0 = 128
LINK_ROWS = 176
CHUNKS = 1
MESH = pl.DeviceIdType.MESH


def exchange_kernel(tr_hbm, ec_hbm, nc_hbm, flux_hbm, src_hbm, wgt_hbm, tgt_hbm,
                    surf_ref, pe_ref, pw_ref, south_ref, north_ref, ncs_ref,
                    T, EC, NC, flux_ref, src_ref, wgt_ref, tgt_ref,
                    L, RL, TG, WPa, WPb, TAa, TAb, TBa, TBb, Za, Zb, Ba, Bb, ACC, Q, pe_out, pw_out, rows_out, nc_out, load_sem, send_sem, recv_sem):
    rows, cols = 128, 128
    lat, lon = lax.axis_index("lat"), lax.axis_index("lon")
    nlat, nlon = lax.axis_size("lat"), lax.axis_size("lon")
    north, south = lax.rem(lat + 1, nlat), lax.rem(lat + nlat - 1, nlat)
    east, west = lax.rem(lon + 1, nlon), lax.rem(lon + nlon - 1, nlon)

    loads = [
        pltpu.make_async_copy(src_hbm, src_ref, load_sem.at[0]),
        pltpu.make_async_copy(wgt_hbm, wgt_ref, load_sem.at[1]),
        pltpu.make_async_copy(flux_hbm, flux_ref, load_sem.at[2]),
        pltpu.make_async_copy(tgt_hbm, tgt_ref, load_sem.at[3]),
        pltpu.make_async_copy(tr_hbm, T, load_sem.at[4]),
        pltpu.make_async_copy(ec_hbm, EC, load_sem.at[5]),
        pltpu.make_async_copy(nc_hbm.at[:, rows - 8:rows, :], NC, load_sem.at[6]),
    ]
    for c in loads:
        c.start()

    barrier = pltpu.get_barrier_semaphore()
    for peer in ((lat, east), (lat, west), (north, lon), (south, lon), (north, east), (south, west)):
        pl.semaphore_signal(barrier, inc=1, device_id=peer, device_id_type=MESH)

    for c in loads[:4]:
        c.wait()
    field = lax.broadcasted_iota(jnp.int32, (8, cols), 0)
    for n in range(4):
        for h in range(16):
            lanes = pl.ds(n * 2048 + h * 128, 128)
            tile = flux_ref[0:6, lanes]
            more = jnp.where(field[0:5] == 1, jnp.broadcast_to(tile[5:6], (5, cols)), 0.0)
            L[n, h * FIELDS:(h + 1) * FIELDS, :] = tile[0:5] + more
        for j in range(CAP_ROWS):
            lanes = pl.ds(j * 128, 128)
            L[n, SRC0 + j:SRC0 + j + 1, :] = (src_ref[0, n:n + 1, lanes] - n * 2048).astype(jnp.float32)
            L[n, WGT0 + j:WGT0 + j + 1, :] = wgt_ref[0, n:n + 1, lanes]
            TG[n, j:j + 1, :] = tgt_ref[0, n:n + 1, lanes]

    pl.semaphore_wait(barrier, 6)

    def send(src, dst, at, peer):
        copy = pltpu.make_async_remote_copy(
            src_ref=src, dst_ref=dst, send_sem=send_sem.at[at], recv_sem=recv_sem.at[at],
            device_id=peer, device_id_type=MESH)
        copy.start()
        return copy

    links = {
        1: send(L.at[1], RL.at[0], 0, (lat, east)),
        2: send(L.at[2], RL.at[1], 1, (north, lon)),
        3: send(L.at[3], RL.at[2], 2, (north, east)),
    }

    b16 = jnp.bfloat16
    sub16 = lax.broadcasted_iota(jnp.int32, (16, cols), 0).astype(jnp.float32)
    subs = [(sub16 + 16.0 * s).astype(b16) for s in range(16)]
    one, zero16 = jnp.ones((16, cols), b16), jnp.zeros((16, cols), b16)

    def pick(n, box, WP, TA, TB, g):
        exists = jnp.where(lat >= n // 2, 1.0, 0.0)
        at = pl.ds(pl.multiple_of(g * 8, 8), 8)
        target = TG[n, at, :]
        row = (target >> 7) & 63
        TA[at, :] = (row >> 2).astype(jnp.float32)
        TB[at, :] = (((row & 3) << 6) + (target & 63)).astype(jnp.float32)
        cell = box[pl.ds(pl.multiple_of(SRC0 + g * 8, 8), 8), :].astype(jnp.int32)
        weight = box[pl.ds(pl.multiple_of(WGT0 + g * 8, 8), 8), :] * exists
        low = cell & 127
        high = cell >> 7
        for f in range(FIELDS):
            got = jnp.zeros((8, cols), jnp.float32)
            for h in range(16):
                line = jnp.broadcast_to(box[h * FIELDS + f:h * FIELDS + f + 1, :], (8, cols))
                got = jnp.where(high == h, jnp.take_along_axis(line, low, axis=1), got)
            got = got * weight
            top = got.astype(b16).astype(jnp.float32)
            WP[f, at, :] = top
            WP[FIELDS + f, at, :] = got - top

    def hot(WP, TA, TB, Z, B, g):
        for u in range(8):
            j = g * 8 + u
            lanes = pl.ds(pl.multiple_of(j * 128, 128), 128)
            a = jnp.broadcast_to(TA[pl.ds(j, 1), :], (16, cols)).astype(b16) == subs[0]
            b = jnp.broadcast_to(TB[pl.ds(j, 1), :], (16, cols)).astype(b16)
            for w in range(2 * FIELDS):
                v = jnp.broadcast_to(WP[w, pl.ds(j, 1), :], (16, cols)).astype(b16)
                Z[w * 16:(w + 1) * 16, lanes] = jnp.where(a, v, zero16)
            for s in range(16):
                B[s * 16:(s + 1) * 16, lanes] = jnp.where(b == subs[s], one, zero16)

    def place(Z, B, g):
        size = CAP_ROWS * 128 // CHUNKS
        lanes = pl.ds(pl.multiple_of(g * size, size), size)
        return lax.dot_general(Z[:, lanes], B[:, lanes], (((1,), (1,)), ((), ())), preferred_element_type=jnp.float32)

    def spread(n):
        col0 = (1 - n % 2) * 64
        for f in range(FIELDS):
            total = ACC[f * 16:(f + 1) * 16, :] + ACC[(FIELDS + f) * 16:(FIELDS + f + 1) * 16, :]
            for i in range(4):
                part = total[:, (i // 2) * 128:(i // 2 + 1) * 128]
                if (i % 2) * 64 != col0:
                    part = pltpu.roll(part, 64, 1)
                Q[n, f, i] = part

    order = (0, 2, 1, 3)
    boxes = {0: L.at[0], 1: RL.at[0], 2: RL.at[1], 3: RL.at[2]}
    words = ((WPa, TAa, TBa), (WPb, TAb, TBb))
    hots = ((Za, Ba), (Zb, Bb))

    def stage(i):
        def body(g, carry):
            if 0 <= i - 2 < 4:
                part = place(*hots[i % 2], g)
            for v in range(6 // CHUNKS):
                if 0 <= i - 1 < 4:
                    hot(*words[(i - 1) % 2], *hots[(i - 1) % 2], g * (6 // CHUNKS) + v)
                if i < 4:
                    pick(order[i], boxes[order[i]], *words[i % 2], g * (6 // CHUNKS) + v)
            if 0 <= i - 2 < 4:
                ACC[...] += part
            return carry

        if 0 <= i - 2 < 4:
            ACC[...] = jnp.zeros(ACC.shape, jnp.float32)
        lax.fori_loop(0, CHUNKS, body, 0)
        if 0 <= i - 2 < 4:
            spread(order[i - 2])

    stage(0)

    for c in loads[4:]:
        c.wait()
    lane = lax.broadcasted_iota(jnp.int32, (64, cols), 1)
    for t in range(2):
        for z in range(2):
            rr = pl.ds(z * 64, 64)

            def pack(q, carry):
                pe, pw = carry
                for u in range(8):
                    k = q * 8 + u
                    half = k // HALF
                    j = k - half * HALF
                    by = 4 * j + 2 * (1 - half)
                    y = pltpu.roll(T[t, k, rr, :], by, 1)
                    off = (lane - by) & 127
                    pe = jnp.where(off < 2, y, pe)
                    pw = jnp.where(off >= 126, y, pw)
                return pe, pw

            zero = jnp.zeros((64, cols), jnp.float32)
            pe, pw = lax.fori_loop(0, LEVELS // 8, pack, (zero, zero))

            def pack_courant(q, pw):
                for u in range(8):
                    j = q * 8 + u
                    y = pltpu.roll(EC[t * HALF + j, rr, :], j + 97, 1)
                    pw = jnp.where(lane == 96 + j, y, pw)
                return pw

            pw = lax.fori_loop(0, HALF // 8, pack_courant, pw)
            pe_out[t, rr, :] = pe
            pw_out[t, rr, :] = pw

    def edge_rows(k, carry):
        for t in range(2):
            rows_out[0, t, k] = T[t, k, 0:2, :]
            rows_out[1, t, k] = T[t, k, rows - 2:rows, :]
        nc_out[k] = NC[k, 7:8, :]
        return carry

    lax.fori_loop(0, LEVELS, edge_rows, 0)

    halos = [
        send(pe_out, pe_ref, 3, (lat, west)),
        send(pw_out, pw_ref, 4, (lat, east)),
        send(rows_out.at[0], north_ref, 5, (south, lon)),
        send(rows_out.at[1], south_ref, 6, (north, lon)),
        send(nc_out, ncs_ref, 7, (north, lon)),
    ]

    for i in range(1, 6):
        if i < 4:
            links[order[i]].wait()
        stage(i)

    left = lax.broadcasted_iota(jnp.int32, (16, cols), 1) < 64
    for a in range(2):
        for f in range(FIELDS):
            for i in range(4):
                surf_ref[f, pl.ds((1 - a) * 64 + i, 16, stride=4), :] = jnp.where(left, Q[2 * a + 1, f, i], Q[2 * a, f, i])

    for c in halos:
        c.wait()
    below = jnp.where(lat > 0, 1.0, 0.0)
    over = jnp.where(lat < nlat - 1, 1.0, 0.0)
    south_ref[...] = south_ref[...] * below
    ncs_ref[...] = ncs_ref[...] * below
    north_ref[...] = north_ref[...] * over


def exchange(tracers, ec, nc, fluxes, source_cell, link_weight, target_cell):
    hbm = pl.BlockSpec(memory_space=pltpu.HBM)
    vm = pl.BlockSpec(memory_space=pltpu.VMEM)
    f = jnp.float32
    s = jax.ShapeDtypeStruct
    return pl.pallas_call(
        exchange_kernel,
        out_shape=[s((FIELDS, 128, 128), f), s((2, 128, 128), f), s((2, 128, 128), f), s((2, LEVELS, 2, 128), f),
                   s((2, LEVELS, 2, 128), f), s((LEVELS, 1, 128), f)],
        in_specs=[hbm] * 7,
        out_specs=[vm] * 6,
        scratch_shapes=[
            pltpu.VMEM((2, LEVELS, 128, 128), f),
            pltpu.VMEM((LEVELS, 128, 128), f),
            pltpu.VMEM((LEVELS, 8, 128), f),
            pltpu.VMEM((6, 8192), f),
            pltpu.VMEM((1, 4, 6144), jnp.int32),
            pltpu.VMEM((1, 4, 6144), f),
            pltpu.VMEM((1, 4, 6144), jnp.int32),
            pltpu.VMEM((4, LINK_ROWS, 128), f),
            pltpu.VMEM((3, LINK_ROWS, 128), f),
            pltpu.VMEM((4, CAP_ROWS, 128), jnp.int32),
            pltpu.VMEM((2 * FIELDS, CAP_ROWS, 128), f),
            pltpu.VMEM((2 * FIELDS, CAP_ROWS, 128), f),
            pltpu.VMEM((CAP_ROWS, 128), f),
            pltpu.VMEM((CAP_ROWS, 128), f),
            pltpu.VMEM((CAP_ROWS, 128), f),
            pltpu.VMEM((CAP_ROWS, 128), f),
            pltpu.VMEM((2 * FIELDS * 16, 6144), jnp.bfloat16),
            pltpu.VMEM((2 * FIELDS * 16, 6144), jnp.bfloat16),
            pltpu.VMEM((256, 6144), jnp.bfloat16),
            pltpu.VMEM((256, 6144), jnp.bfloat16),
            pltpu.VMEM((2 * FIELDS * 16, 256), f),
            pltpu.VMEM((4, FIELDS, 4, 16, 128), f),
            pltpu.VMEM((2, 128, 128), f),
            pltpu.VMEM((2, 128, 128), f),
            pltpu.VMEM((2, 2, LEVELS, 2, 128), f),
            pltpu.VMEM((LEVELS, 1, 128), f),
            pltpu.SemaphoreType.DMA((7,)),
            pltpu.SemaphoreType.DMA((8,)),
            pltpu.SemaphoreType.DMA((8,)),
        ],
        compiler_params=pltpu.CompilerParams(collective_id=0, has_side_effects=True, vmem_limit_bytes=60 << 20),
        name="exchange",
    )(tracers, ec, nc, fluxes, source_cell, link_weight, target_cell)


def local(tracers, east_courant, north_courant, diffusivity, land_sea, fluxes, source_cell, link_weight, target_cell):
    surf, pe, pw, south, north, ncs = exchange(
        tracers, east_courant, north_courant, fluxes, source_cell, link_weight, target_cell)
    return column_step(tracers, east_courant, north_courant, diffusivity, land_sea, surf, pe, pw, south, north, ncs)


def solution(mesh):
    in_specs = (
        P(None, None, "lat", "lon"),
        P(None, "lat", "lon"),
        P(None, "lat", "lon"),
        P(None, "lat", "lon"),
        P("lat", "lon"),
        P(None, ("lat", "lon")),
        P(("lat", "lon"), None, None),
        P(("lat", "lon"), None, None),
        P(("lat", "lon"), None, None),
    )
    out_specs = P(None, None, "lat", "lon")
    return jax.shard_map(local, mesh=mesh, in_specs=in_specs, out_specs=out_specs, check_vma=False)
```

```python
import math
import jax, jax.numpy as jnp
import numpy as np
from jax import lax
from jax.experimental import pallas as pl
from jax.experimental.pallas import tpu as pltpu
from jax.sharding import PartitionSpec as P

LEVELS = 48
HALF = 24
R = 32
G = 12
PAD = 8


def stencil_weights():
    cols = 128
    main = np.zeros((cols, 2 * cols), np.float32)
    for i in range(cols):
        for off, w in ((-1, -1), (0, 7), (1, 7), (2, -1)):
            if 0 <= i + off < cols:
                main[i + off, i] = w
        for off, w in ((-2, -1), (-1, 7), (0, 7), (1, -1)):
            if 0 <= i + off < cols:
                main[i + off, cols + i] = w
    halves = []
    for half in range(2):
        edge = np.zeros((cols, 2 * cols), np.float32)
        order = (-2, -1, 128, 129) if half == 0 else (128, 129, -2, -1)
        for lane in range(cols):
            p = order[lane % 4]
            for i in range(cols):
                edge[lane, i] = {-1: -1, 0: 7, 1: 7, 2: -1}.get(p - i, 0)
                edge[lane, cols + i] = {-2: -1, -1: 7, 0: 7, 1: -1}.get(p - i, 0)
        halves.append(np.concatenate([main, main, edge, edge], 0))
    return jnp.asarray(np.stack(halves), jnp.bfloat16)


def two_pieces(x):
    high = x.astype(jnp.bfloat16)
    return high, (x - high.astype(jnp.float32)).astype(jnp.bfloat16)


def column_kernel(tr_hbm, ec_hbm, nc_hbm, df_hbm, w_ref, land_ref, surf_ref, pe_ref, pw_ref, south_ref, north_ref, ncs_ref,
                  out_hbm, T, EC, NC, DF, C, OUT, H, X, S, FN, tr_sem, co_sem, df_sem, out_sem):
    rows, cols = 128, 128
    blocks = rows // R

    groups = LEVELS // G

    def span(i, size):
        return pl.ds(pl.multiple_of(i * size, size), size)

    def load_tracers(b, g):
        return pltpu.make_async_copy(
            tr_hbm.at[:, span(g, G), span(b, R), :],
            T.at[:, span(g, G), pl.ds(pl.multiple_of(b * R + PAD, PAD), R), :], tr_sem.at[b, g])

    def load_courants(b, g):
        return [pltpu.make_async_copy(h.at[span(g, G), span(b, R), :], v.at[span(g, G), span(b, R), :], co_sem.at[p, b, g])
                for p, (h, v) in enumerate(((ec_hbm, EC), (nc_hbm, NC)))]

    def load_diffusivity(b):
        return pltpu.make_async_copy(df_hbm.at[:, span(b, R), :], DF.at[:, span(b, R), :], df_sem.at[b])

    def start_block(b, carry):
        def start_group(g, carry):
            @pl.when(b == 0)
            def _():
                load_tracers(0, g).start()

            @pl.when(b + 1 < blocks)
            def _():
                load_tracers(b + 1, g).start()

            for c in load_courants(b, g):
                c.start()
            return carry

        lax.fori_loop(0, groups, start_group, 0)
        load_diffusivity(b).start()
        return carry

    lax.fori_loop(0, blocks, start_block, 0)

    lane = lax.broadcasted_iota(jnp.int32, (rows, cols), 1)
    low = lane % 4 < 2
    for t in range(2):
        pe, pw = pe_ref[t], pw_ref[t]
        for half in range(2):
            h = jnp.where(low, pw, pe) if half == 0 else jnp.where(low, pe, pw)
            H[t, half, 0], H[t, half, 1] = two_pieces(h)

    def pad_rows(k, carry):
        for t in range(2):
            T[t, k, PAD - 2:PAD, :] = south_ref[t, k]
            T[t, k, PAD + rows:PAD + rows + 2, :] = north_ref[t, k]
        return carry

    lax.fori_loop(0, LEVELS, pad_rows, 0)

    def block(b, carry):
        r = pl.multiple_of(b * R, R)
        rr = pl.ds(r, R)
        lane = lax.broadcasted_iota(jnp.int32, (R, cols), 1)
        first = lane == 0
        stress = 2.0 * jnp.sqrt(surf_ref[3, rr, :] * surf_ref[3, rr, :] + surf_ref[4, rr, :] * surf_ref[4, rr, :])

        for half in range(2):
            def group(q, carry):
                g = half * (HALF // G) + q

                @pl.when(b == 0)
                def _():
                    load_tracers(0, g).wait()

                @pl.when(b + 1 < blocks)
                def _():
                    load_tracers(b + 1, g).wait()

                for c in load_courants(b, g):
                    c.wait()

                @pl.when(b == 0)
                def _():
                    for u in range(G):
                        k = g * G + u
                        for t in range(2):
                            s = T[t, k, PAD - 2:PAD - 1, :] + T[t, k, PAD + 1:PAD + 2, :]
                            m = T[t, k, PAD - 1:PAD, :] + T[t, k, PAD:PAD + 1, :]
                            FN[t, k, PAD - 1:PAD, :] = ncs_ref[k] * (7.0 * m - s)

                for u in range(G):
                    j = q * G + u
                    k = half * HALF + j
                    here = ((lane + 2 * half) & (cols - 1)) >> 2 == j
                    for t in range(2):
                        x = T[t, k, pl.ds(r + PAD, R), :]
                        at = pl.ds((u * 2 + t) * R, R)
                        X[at, 0:cols], X[at, cols:2 * cols] = two_pieces(x)
                        for p in range(2):
                            h = H[t, half, p, rr, :]
                            X[at, (2 + p) * cols:(3 + p) * cols] = jnp.where(here, h, jnp.zeros_like(h))
                S[...] = jnp.dot(X[...], w_ref[half], preferred_element_type=jnp.float32)
                for u in range(G):
                    j = q * G + u
                    k = half * HALF + j
                    ce = EC[k, rr, :]
                    cn = NC[k, rr, :]
                    hec = pltpu.roll(pw_ref[half, rr, :], cols - 96 - j, 1)
                    cw = jnp.where(first, hec, pltpu.roll(ce, 1, 1))
                    for t in range(2):
                        at = pl.ds((u * 2 + t) * R, R)
                        x = T[t, k, pl.ds(r + PAD, R), :]
                        n1 = T[t, k, pl.ds(r + PAD + 1, R), :]
                        n2 = T[t, k, pl.ds(r + PAD + 2, R), :]
                        s1 = T[t, k, pl.ds(r + PAD - 1, R), :]
                        fn = cn * (7.0 * (x + n1) - (s1 + n2))
                        FN[t, k, pl.ds(r + PAD, R), :] = fn
                        fs = FN[t, k, pl.ds(r + PAD - 1, R), :]
                        div = (ce * S[at, 0:cols] - cw * S[at, cols:2 * cols]) + (fn - fs)
                        OUT[t, k, rr, :] = x - div * (1.0 / 12.0)
                return carry

            lax.fori_loop(0, HALF // G, group, 0)

        load_diffusivity(b).wait()
        heat = 0.5 * surf_ref[2, rr, :]
        tops = [0.5 * surf_ref[0, rr, :], 0.5 * surf_ref[1, rr, :]]
        above = None
        cprev = None
        vprev = [None, None]
        for k in range(LEVELS):
            if k < LEVELS - 1:
                below = DF[k, rr, :] + stress * math.exp(-4.0 * k / LEVELS)
            absorb = math.exp(-4.0 * k / LEVELS) - math.exp(-4.0 * (k + 1) / LEVELS)
            adv = [OUT[0, k, rr, :] + heat * absorb, OUT[1, k, rr, :]]
            if k == 0:
                adv[0] = adv[0] + tops[0]
                adv[1] = adv[1] + tops[1]
                inv = 1.0 / (1.0 + below)
                v = [adv[0] * inv, adv[1] * inv]
            else:
                pivot = 1.0 + above * (1.0 - cprev)
                if k < LEVELS - 1:
                    pivot = pivot + below
                inv = 1.0 / pivot
                v = [(adv[t] + above * vprev[t]) * inv for t in range(2)]
            if k < LEVELS - 1:
                cprev = below * inv
                C[k] = cprev
                above = below
                for t in range(2):
                    OUT[t, k, rr, :] = v[t]
            vprev = v
        sea = land_ref[rr, :] == 1
        x = vprev
        for k in range(LEVELS - 1, -1, -1):
            if k < LEVELS - 1:
                c = C[k]
                x = [OUT[t, k, rr, :] + c * x[t] for t in range(2)]
            for t in range(2):
                OUT[t, k, rr, :] = jnp.where(sea, x[t], T[t, k, pl.ds(r + PAD, R), :])
        pltpu.make_async_copy(OUT.at[:, :, rr, :], out_hbm.at[:, :, rr, :], out_sem.at[b]).start()
        return carry

    lax.fori_loop(0, blocks, block, 0)

    def drain(b, carry):
        rr = pl.ds(pl.multiple_of(b * R, R), R)
        pltpu.make_async_copy(OUT.at[:, :, rr, :], out_hbm.at[:, :, rr, :], out_sem.at[b]).wait()
        return carry

    lax.fori_loop(0, blocks, drain, 0)


def column_step(tracers, ec, nc, df, land, surf, pe, pw, south, north, ncs):
    any_ = pl.BlockSpec(memory_space=pltpu.HBM)
    vm = pl.BlockSpec(memory_space=pltpu.VMEM)
    blocks = 128 // R
    f = jnp.float32
    return pl.pallas_call(
        column_kernel,
        out_shape=jax.ShapeDtypeStruct(tracers.shape, f),
        in_specs=[any_] * 4 + [vm] * 8,
        out_specs=any_,
        scratch_shapes=[
            pltpu.VMEM((2, LEVELS, 144, 128), f),
            pltpu.VMEM((LEVELS, 128, 128), f),
            pltpu.VMEM((LEVELS, 128, 128), f),
            pltpu.VMEM((LEVELS, 128, 128), f),
            pltpu.VMEM((LEVELS, R, 128), f),
            pltpu.VMEM((2, LEVELS, 128, 128), f),
            pltpu.VMEM((2, 2, 2, 128, 128), jnp.bfloat16),
            pltpu.VMEM((2 * G * R, 512), jnp.bfloat16),
            pltpu.VMEM((2 * G * R, 256), f),
            pltpu.VMEM((2, LEVELS, 136, 128), f),
            pltpu.SemaphoreType.DMA((blocks, LEVELS // G)),
            pltpu.SemaphoreType.DMA((2, blocks, LEVELS // G)),
            pltpu.SemaphoreType.DMA((blocks,)),
            pltpu.SemaphoreType.DMA((blocks,)),
        ],
        compiler_params=pltpu.CompilerParams(vmem_limit_bytes=60 << 20),
        name="column_step",
    )(tracers, ec, nc, df, stencil_weights(), land, surf, pe, pw, south, north, ncs)
FIELDS = 5
CAP_ROWS = 48
SRC0 = 80
WGT0 = 128
LINK_ROWS = 176
MESH = pl.DeviceIdType.MESH


def exchange_kernel(tr_hbm, ec_hbm, nc_hbm, flux_hbm, src_hbm, wgt_hbm, tgt_hbm,
                    surf_ref, pe_ref, pw_ref, south_ref, north_ref, ncs_ref,
                    T, EC, NC, flux_ref, src_ref, wgt_ref, tgt_ref,
                    L, RL, TG, WPa, WPb, TAa, TAb, TBa, TBb, Za, Zb, Ba, Bb, ACC, Q, pe_out, pw_out, rows_out, nc_out, load_sem, send_sem, recv_sem):
    rows, cols = 128, 128
    lat, lon = lax.axis_index("lat"), lax.axis_index("lon")
    nlat, nlon = lax.axis_size("lat"), lax.axis_size("lon")
    north, south = lax.rem(lat + 1, nlat), lax.rem(lat + nlat - 1, nlat)
    east, west = lax.rem(lon + 1, nlon), lax.rem(lon + nlon - 1, nlon)

    loads = [
        pltpu.make_async_copy(src_hbm, src_ref, load_sem.at[0]),
        pltpu.make_async_copy(wgt_hbm, wgt_ref, load_sem.at[1]),
        pltpu.make_async_copy(flux_hbm, flux_ref, load_sem.at[2]),
        pltpu.make_async_copy(tgt_hbm, tgt_ref, load_sem.at[3]),
        pltpu.make_async_copy(tr_hbm, T, load_sem.at[4]),
        pltpu.make_async_copy(ec_hbm, EC, load_sem.at[5]),
        pltpu.make_async_copy(nc_hbm.at[:, rows - 8:rows, :], NC, load_sem.at[6]),
    ]
    for c in loads:
        c.start()

    barrier = pltpu.get_barrier_semaphore()
    for peer in ((lat, east), (lat, west), (north, lon), (south, lon), (north, east), (south, west)):
        pl.semaphore_signal(barrier, inc=1, device_id=peer, device_id_type=MESH)

    for c in loads[:4]:
        c.wait()
    field = lax.broadcasted_iota(jnp.int32, (8, cols), 0)
    for n in range(4):
        for h in range(16):
            lanes = pl.ds(n * 2048 + h * 128, 128)
            tile = flux_ref[0:6, lanes]
            more = jnp.where(field[0:5] == 1, jnp.broadcast_to(tile[5:6], (5, cols)), 0.0)
            L[n, h * FIELDS:(h + 1) * FIELDS, :] = tile[0:5] + more
        for j in range(CAP_ROWS):
            lanes = pl.ds(j * 128, 128)
            L[n, SRC0 + j:SRC0 + j + 1, :] = (src_ref[0, n:n + 1, lanes] - n * 2048).astype(jnp.float32)
            L[n, WGT0 + j:WGT0 + j + 1, :] = wgt_ref[0, n:n + 1, lanes]
            TG[n, j:j + 1, :] = tgt_ref[0, n:n + 1, lanes]

    b16 = jnp.bfloat16
    sub16 = lax.broadcasted_iota(jnp.int32, (16, cols), 0).astype(jnp.float32)
    subs = [(sub16 + 16.0 * s).astype(b16) for s in range(16)]
    one, zero16 = jnp.ones((16, cols), b16), jnp.zeros((16, cols), b16)

    def pick(n, box, WP, TA, TB, g):
        exists = jnp.where(lat >= n // 2, 1.0, 0.0)
        at = pl.ds(pl.multiple_of(g * 8, 8), 8)
        target = TG[n, at, :]
        row = (target >> 7) & 63
        TA[at, :] = (row >> 2).astype(jnp.float32)
        TB[at, :] = (((row & 3) << 6) + (target & 63)).astype(jnp.float32)
        cell = box[pl.ds(pl.multiple_of(SRC0 + g * 8, 8), 8), :].astype(jnp.int32)
        weight = box[pl.ds(pl.multiple_of(WGT0 + g * 8, 8), 8), :] * exists
        low = cell & 127
        high = cell >> 7
        for f in range(FIELDS):
            got = jnp.zeros((8, cols), jnp.float32)
            for h in range(16):
                line = jnp.broadcast_to(box[h * FIELDS + f:h * FIELDS + f + 1, :], (8, cols))
                got = jnp.where(high == h, jnp.take_along_axis(line, low, axis=1), got)
            got = got * weight
            top = got.astype(b16).astype(jnp.float32)
            WP[f, at, :] = top
            WP[FIELDS + f, at, :] = got - top

    def hot(WP, TA, TB, Z, B, g):
        for u in range(8):
            j = g * 8 + u
            lanes = pl.ds(pl.multiple_of(j * 128, 128), 128)
            a = jnp.broadcast_to(TA[pl.ds(j, 1), :], (16, cols)).astype(b16) == subs[0]
            b = jnp.broadcast_to(TB[pl.ds(j, 1), :], (16, cols)).astype(b16)
            for w in range(2 * FIELDS):
                v = jnp.broadcast_to(WP[w, pl.ds(j, 1), :], (16, cols)).astype(b16)
                Z[w * 16:(w + 1) * 16, lanes] = jnp.where(a, v, zero16)
            for s in range(16):
                B[s * 16:(s + 1) * 16, lanes] = jnp.where(b == subs[s], one, zero16)

    def place(Z, B, g):
        size = CAP_ROWS * 128
        lanes = pl.ds(pl.multiple_of(g * size, size), size)
        return lax.dot_general(Z[:, lanes], B[:, lanes], (((1,), (1,)), ((), ())), preferred_element_type=jnp.float32)

    def spread(n):
        col0 = (1 - n % 2) * 64
        for f in range(FIELDS):
            total = ACC[f * 16:(f + 1) * 16, :] + ACC[(FIELDS + f) * 16:(FIELDS + f + 1) * 16, :]
            for i in range(4):
                part = total[:, (i // 2) * 128:(i // 2 + 1) * 128]
                if (i % 2) * 64 != col0:
                    part = pltpu.roll(part, 64, 1)
                Q[n, f, i] = part

    order = (0, 2, 1, 3)
    boxes = {0: L.at[0], 1: RL.at[0], 2: RL.at[1], 3: RL.at[2]}
    words = ((WPa, TAa, TBa), (WPb, TAb, TBb))
    hots = ((Za, Ba), (Zb, Bb))

    def stage(picked, hotted, placed):
        def body(g, carry):
            if placed is not None:
                ACC[...] = place(*hots[placed % 2], g)
            for v in range(CAP_ROWS // 8):
                if hotted is not None:
                    hot(*words[hotted % 2], *hots[hotted % 2], v)
                if picked is not None:
                    pick(order[picked], boxes[order[picked]], *words[picked % 2], v)
            return carry

        lax.fori_loop(0, 1, body, 0)
        if placed is not None:
            spread(order[placed])

    stage(0, None, None)
    stage(None, 0, None)

    pl.semaphore_wait(barrier, 6)

    def send(src, dst, at, peer):
        copy = pltpu.make_async_remote_copy(
            src_ref=src, dst_ref=dst, send_sem=send_sem.at[at], recv_sem=recv_sem.at[at],
            device_id=peer, device_id_type=MESH)
        copy.start()
        return copy

    links = {
        1: send(L.at[1], RL.at[0], 0, (lat, east)),
        2: send(L.at[2], RL.at[1], 1, (north, lon)),
        3: send(L.at[3], RL.at[2], 2, (north, east)),
    }


    for c in loads[4:]:
        c.wait()
    lane = lax.broadcasted_iota(jnp.int32, (64, cols), 1)
    for t in range(2):
        for z in range(2):
            rr = pl.ds(z * 64, 64)

            def pack(q, carry):
                pe, pw = carry
                for u in range(8):
                    k = q * 8 + u
                    half = k // HALF
                    j = k - half * HALF
                    by = 4 * j + 2 * (1 - half)
                    y = pltpu.roll(T[t, k, rr, :], by, 1)
                    off = (lane - by) & 127
                    pe = jnp.where(off < 2, y, pe)
                    pw = jnp.where(off >= 126, y, pw)
                return pe, pw

            zero = jnp.zeros((64, cols), jnp.float32)
            pe, pw = lax.fori_loop(0, LEVELS // 8, pack, (zero, zero))

            def pack_courant(q, pw):
                for u in range(8):
                    j = q * 8 + u
                    y = pltpu.roll(EC[t * HALF + j, rr, :], j + 97, 1)
                    pw = jnp.where(lane == 96 + j, y, pw)
                return pw

            pw = lax.fori_loop(0, HALF // 8, pack_courant, pw)
            pe_out[t, rr, :] = pe
            pw_out[t, rr, :] = pw

    def edge_rows(k, carry):
        for t in range(2):
            rows_out[0, t, k] = T[t, k, 0:2, :]
            rows_out[1, t, k] = T[t, k, rows - 2:rows, :]
        nc_out[k] = NC[k, 7:8, :]
        return carry

    lax.fori_loop(0, LEVELS, edge_rows, 0)

    halos = [
        send(pe_out, pe_ref, 3, (lat, west)),
        send(pw_out, pw_ref, 4, (lat, east)),
        send(rows_out.at[0], north_ref, 5, (south, lon)),
        send(rows_out.at[1], south_ref, 6, (north, lon)),
        send(nc_out, ncs_ref, 7, (north, lon)),
    ]

    links[order[1]].wait()
    stage(1, None, 0)
    links[order[2]].wait()
    stage(2, 1, None)
    links[order[3]].wait()
    stage(3, 2, 1)
    stage(None, 3, 2)
    stage(None, None, 3)

    left = lax.broadcasted_iota(jnp.int32, (16, cols), 1) < 64
    for a in range(2):
        for f in range(FIELDS):
            for i in range(4):
                surf_ref[f, pl.ds((1 - a) * 64 + i, 16, stride=4), :] = jnp.where(left, Q[2 * a + 1, f, i], Q[2 * a, f, i])

    for c in halos:
        c.wait()
    below = jnp.where(lat > 0, 1.0, 0.0)
    over = jnp.where(lat < nlat - 1, 1.0, 0.0)
    south_ref[...] = south_ref[...] * below
    ncs_ref[...] = ncs_ref[...] * below
    north_ref[...] = north_ref[...] * over


def exchange(tracers, ec, nc, fluxes, source_cell, link_weight, target_cell):
    hbm = pl.BlockSpec(memory_space=pltpu.HBM)
    vm = pl.BlockSpec(memory_space=pltpu.VMEM)
    f = jnp.float32
    s = jax.ShapeDtypeStruct
    return pl.pallas_call(
        exchange_kernel,
        out_shape=[s((FIELDS, 128, 128), f), s((2, 128, 128), f), s((2, 128, 128), f), s((2, LEVELS, 2, 128), f),
                   s((2, LEVELS, 2, 128), f), s((LEVELS, 1, 128), f)],
        in_specs=[hbm] * 7,
        out_specs=[vm] * 6,
        scratch_shapes=[
            pltpu.VMEM((2, LEVELS, 128, 128), f),
            pltpu.VMEM((LEVELS, 128, 128), f),
            pltpu.VMEM((LEVELS, 8, 128), f),
            pltpu.VMEM((6, 8192), f),
            pltpu.VMEM((1, 4, 6144), jnp.int32),
            pltpu.VMEM((1, 4, 6144), f),
            pltpu.VMEM((1, 4, 6144), jnp.int32),
            pltpu.VMEM((4, LINK_ROWS, 128), f),
            pltpu.VMEM((3, LINK_ROWS, 128), f),
            pltpu.VMEM((4, CAP_ROWS, 128), jnp.int32),
            pltpu.VMEM((2 * FIELDS, CAP_ROWS, 128), f),
            pltpu.VMEM((2 * FIELDS, CAP_ROWS, 128), f),
            pltpu.VMEM((CAP_ROWS, 128), f),
            pltpu.VMEM((CAP_ROWS, 128), f),
            pltpu.VMEM((CAP_ROWS, 128), f),
            pltpu.VMEM((CAP_ROWS, 128), f),
            pltpu.VMEM((2 * FIELDS * 16, 6144), jnp.bfloat16),
            pltpu.VMEM((2 * FIELDS * 16, 6144), jnp.bfloat16),
            pltpu.VMEM((256, 6144), jnp.bfloat16),
            pltpu.VMEM((256, 6144), jnp.bfloat16),
            pltpu.VMEM((2 * FIELDS * 16, 256), f),
            pltpu.VMEM((4, FIELDS, 4, 16, 128), f),
            pltpu.VMEM((2, 128, 128), f),
            pltpu.VMEM((2, 128, 128), f),
            pltpu.VMEM((2, 2, LEVELS, 2, 128), f),
            pltpu.VMEM((LEVELS, 1, 128), f),
            pltpu.SemaphoreType.DMA((7,)),
            pltpu.SemaphoreType.DMA((8,)),
            pltpu.SemaphoreType.DMA((8,)),
        ],
        compiler_params=pltpu.CompilerParams(collective_id=0, has_side_effects=True, vmem_limit_bytes=60 << 20),
        name="exchange",
    )(tracers, ec, nc, fluxes, source_cell, link_weight, target_cell)


def local(tracers, east_courant, north_courant, diffusivity, land_sea, fluxes, source_cell, link_weight, target_cell):
    surf, pe, pw, south, north, ncs = exchange(
        tracers, east_courant, north_courant, fluxes, source_cell, link_weight, target_cell)
    return column_step(tracers, east_courant, north_courant, diffusivity, land_sea, surf, pe, pw, south, north, ncs)


def solution(mesh):
    in_specs = (
        P(None, None, "lat", "lon"),
        P(None, "lat", "lon"),
        P(None, "lat", "lon"),
        P(None, "lat", "lon"),
        P("lat", "lon"),
        P(None, ("lat", "lon")),
        P(("lat", "lon"), None, None),
        P(("lat", "lon"), None, None),
        P(("lat", "lon"), None, None),
    )
    out_specs = P(None, None, "lat", "lon")
    return jax.shard_map(local, mesh=mesh, in_specs=in_specs, out_specs=out_specs, check_vma=False)
```

```python
import math
import jax, jax.numpy as jnp
import numpy as np
from jax import lax
from jax.experimental import pallas as pl
from jax.experimental.pallas import tpu as pltpu
from jax.sharding import PartitionSpec as P

LEVELS = 48
HALF = 24
R = 32
G = 12
PAD = 8


def stencil_weights():
    cols = 128
    main = np.zeros((cols, 2 * cols), np.float32)
    for i in range(cols):
        for off, w in ((-1, -1), (0, 7), (1, 7), (2, -1)):
            if 0 <= i + off < cols:
                main[i + off, i] = w
        for off, w in ((-2, -1), (-1, 7), (0, 7), (1, -1)):
            if 0 <= i + off < cols:
                main[i + off, cols + i] = w
    halves = []
    for half in range(2):
        edge = np.zeros((cols, 2 * cols), np.float32)
        order = (-2, -1, 128, 129) if half == 0 else (128, 129, -2, -1)
        for lane in range(cols):
            p = order[lane % 4]
            for i in range(cols):
                edge[lane, i] = {-1: -1, 0: 7, 1: 7, 2: -1}.get(p - i, 0)
                edge[lane, cols + i] = {-2: -1, -1: 7, 0: 7, 1: -1}.get(p - i, 0)
        halves.append(np.concatenate([main, main, edge, edge], 0))
    return jnp.asarray(np.stack(halves), jnp.bfloat16)


def two_pieces(x):
    high = x.astype(jnp.bfloat16)
    return high, (x - high.astype(jnp.float32)).astype(jnp.bfloat16)


def column_kernel(tr_hbm, ec_hbm, nc_hbm, df_hbm, w_hbm, land_hbm, surf_hbm, pe_hbm, pw_hbm, south_hbm, north_hbm, ncs_hbm,
                  out_hbm, w_ref, land_ref, surf_ref, pe_ref, pw_ref, south_ref, north_ref, ncs_ref, T, EC, NC, DF, C, OUT, H, X, S, FN, tr_sem, co_sem, df_sem, out_sem, small_sem):
    rows, cols = 128, 128
    blocks = rows // R

    groups = LEVELS // G

    def span(i, size):
        return pl.ds(pl.multiple_of(i * size, size), size)

    def load_tracers(b, g):
        return pltpu.make_async_copy(
            tr_hbm.at[:, span(g, G), span(b, R), :],
            T.at[:, span(g, G), pl.ds(pl.multiple_of(b * R + PAD, PAD), R), :], tr_sem.at[b, g])

    def load_courants(b, g):
        return [pltpu.make_async_copy(h.at[span(g, G), span(b, R), :], v.at[span(g, G), span(b, R), :], co_sem.at[p, b, g])
                for p, (h, v) in enumerate(((ec_hbm, EC), (nc_hbm, NC)))]

    def load_diffusivity(b):
        return pltpu.make_async_copy(df_hbm.at[:, span(b, R), :], DF.at[:, span(b, R), :], df_sem.at[b])

    def start_block(b, carry):
        def start_group(g, carry):
            @pl.when(b == 0)
            def _():
                load_tracers(0, g).start()

            @pl.when(b + 1 < blocks)
            def _():
                load_tracers(b + 1, g).start()

            for c in load_courants(b, g):
                c.start()
            return carry

        lax.fori_loop(0, groups, start_group, 0)
        load_diffusivity(b).start()
        return carry

    small = [
        pltpu.make_async_copy(h, v, small_sem.at[p]) for p, (h, v) in enumerate((
            (pe_hbm, pe_ref), (pw_hbm, pw_ref), (south_hbm, south_ref), (north_hbm, north_ref), (ncs_hbm, ncs_ref),
            (w_hbm, w_ref), (surf_hbm, surf_ref), (land_hbm, land_ref)))
    ]
    for c in small[:6]:
        c.start()
    start_block(0, 0)
    for c in small[6:]:
        c.start()
    lax.fori_loop(1, blocks, start_block, 0)
    for c in small[:6]:
        c.wait()

    lane = lax.broadcasted_iota(jnp.int32, (rows, cols), 1)
    low = lane % 4 < 2
    for t in range(2):
        pe, pw = pe_ref[t], pw_ref[t]
        for half in range(2):
            h = jnp.where(low, pw, pe) if half == 0 else jnp.where(low, pe, pw)
            H[t, half, 0], H[t, half, 1] = two_pieces(h)

    def pad_rows(k, carry):
        for t in range(2):
            T[t, k, PAD - 2:PAD, :] = south_ref[t, k]
            T[t, k, PAD + rows:PAD + rows + 2, :] = north_ref[t, k]
        return carry

    lax.fori_loop(0, LEVELS, pad_rows, 0)

    def block(b, carry):
        r = pl.multiple_of(b * R, R)
        rr = pl.ds(r, R)
        lane = lax.broadcasted_iota(jnp.int32, (R, cols), 1)
        first = lane == 0

        for half in range(2):
            def group(q, carry):
                g = half * (HALF // G) + q

                @pl.when(b == 0)
                def _():
                    load_tracers(0, g).wait()

                @pl.when(b + 1 < blocks)
                def _():
                    load_tracers(b + 1, g).wait()

                for c in load_courants(b, g):
                    c.wait()

                @pl.when(b == 0)
                def _():
                    for u in range(G):
                        k = g * G + u
                        for t in range(2):
                            s = T[t, k, PAD - 2:PAD - 1, :] + T[t, k, PAD + 1:PAD + 2, :]
                            m = T[t, k, PAD - 1:PAD, :] + T[t, k, PAD:PAD + 1, :]
                            FN[t, k, PAD - 1:PAD, :] = ncs_ref[k] * (7.0 * m - s)

                for u in range(G):
                    j = q * G + u
                    k = half * HALF + j
                    here = ((lane + 2 * half) & (cols - 1)) >> 2 == j
                    for t in range(2):
                        x = T[t, k, pl.ds(r + PAD, R), :]
                        at = pl.ds((u * 2 + t) * R, R)
                        X[at, 0:cols], X[at, cols:2 * cols] = two_pieces(x)
                        for p in range(2):
                            h = H[t, half, p, rr, :]
                            X[at, (2 + p) * cols:(3 + p) * cols] = jnp.where(here, h, jnp.zeros_like(h))
                S[...] = jnp.dot(X[...], w_ref[half], preferred_element_type=jnp.float32)
                for u in range(G):
                    j = q * G + u
                    k = half * HALF + j
                    ce = EC[k, rr, :]
                    cn = NC[k, rr, :]
                    hec = pltpu.roll(pw_ref[half, rr, :], cols - 96 - j, 1)
                    cw = jnp.where(first, hec, pltpu.roll(ce, 1, 1))
                    for t in range(2):
                        at = pl.ds((u * 2 + t) * R, R)
                        x = T[t, k, pl.ds(r + PAD, R), :]
                        n1 = T[t, k, pl.ds(r + PAD + 1, R), :]
                        n2 = T[t, k, pl.ds(r + PAD + 2, R), :]
                        s1 = T[t, k, pl.ds(r + PAD - 1, R), :]
                        fn = cn * (7.0 * (x + n1) - (s1 + n2))
                        FN[t, k, pl.ds(r + PAD, R), :] = fn
                        fs = FN[t, k, pl.ds(r + PAD - 1, R), :]
                        div = (ce * S[at, 0:cols] - cw * S[at, cols:2 * cols]) + (fn - fs)
                        OUT[t, k, rr, :] = x - div * (1.0 / 12.0)
                return carry

            lax.fori_loop(0, HALF // G, group, 0)

        load_diffusivity(b).wait()

        @pl.when(b == 0)
        def _():
            for c in small[6:]:
                c.wait()

        stress = 2.0 * jnp.sqrt(surf_ref[3, rr, :] * surf_ref[3, rr, :] + surf_ref[4, rr, :] * surf_ref[4, rr, :])
        heat = 0.5 * surf_ref[2, rr, :]
        tops = [0.5 * surf_ref[0, rr, :], 0.5 * surf_ref[1, rr, :]]
        above = None
        cprev = None
        vprev = [None, None]
        for k in range(LEVELS):
            if k < LEVELS - 1:
                below = DF[k, rr, :] + stress * math.exp(-4.0 * k / LEVELS)
            absorb = math.exp(-4.0 * k / LEVELS) - math.exp(-4.0 * (k + 1) / LEVELS)
            adv = [OUT[0, k, rr, :] + heat * absorb, OUT[1, k, rr, :]]
            if k == 0:
                adv[0] = adv[0] + tops[0]
                adv[1] = adv[1] + tops[1]
                inv = 1.0 / (1.0 + below)
                v = [adv[0] * inv, adv[1] * inv]
            else:
                pivot = 1.0 + above * (1.0 - cprev)
                if k < LEVELS - 1:
                    pivot = pivot + below
                inv = 1.0 / pivot
                v = [(adv[t] + above * vprev[t]) * inv for t in range(2)]
            if k < LEVELS - 1:
                cprev = below * inv
                C[k] = cprev
                above = below
                for t in range(2):
                    OUT[t, k, rr, :] = v[t]
            vprev = v
        sea = land_ref[rr, :] == 1
        x = vprev
        for k in range(LEVELS - 1, -1, -1):
            if k < LEVELS - 1:
                c = C[k]
                x = [OUT[t, k, rr, :] + c * x[t] for t in range(2)]
            for t in range(2):
                OUT[t, k, rr, :] = jnp.where(sea, x[t], T[t, k, pl.ds(r + PAD, R), :])
        pltpu.make_async_copy(OUT.at[:, :, rr, :], out_hbm.at[:, :, rr, :], out_sem.at[b]).start()
        return carry

    lax.fori_loop(0, blocks, block, 0)

    def drain(b, carry):
        rr = pl.ds(pl.multiple_of(b * R, R), R)
        pltpu.make_async_copy(OUT.at[:, :, rr, :], out_hbm.at[:, :, rr, :], out_sem.at[b]).wait()
        return carry

    lax.fori_loop(0, blocks, drain, 0)


def column_step(tracers, ec, nc, df, land, surf, pe, pw, south, north, ncs):
    any_ = pl.BlockSpec(memory_space=pltpu.HBM)
    blocks = 128 // R
    f = jnp.float32
    return pl.pallas_call(
        column_kernel,
        out_shape=jax.ShapeDtypeStruct(tracers.shape, f),
        in_specs=[any_] * 12,
        out_specs=any_,
        scratch_shapes=[
            pltpu.VMEM((2, 512, 256), jnp.bfloat16),
            pltpu.VMEM((128, 128), jnp.int32),
            pltpu.VMEM((5, 128, 128), f),
            pltpu.VMEM((2, 128, 128), f),
            pltpu.VMEM((2, 128, 128), f),
            pltpu.VMEM((2, LEVELS, 2, 128), f),
            pltpu.VMEM((2, LEVELS, 2, 128), f),
            pltpu.VMEM((LEVELS, 1, 128), f),
            pltpu.VMEM((2, LEVELS, 144, 128), f),
            pltpu.VMEM((LEVELS, 128, 128), f),
            pltpu.VMEM((LEVELS, 128, 128), f),
            pltpu.VMEM((LEVELS, 128, 128), f),
            pltpu.VMEM((LEVELS, R, 128), f),
            pltpu.VMEM((2, LEVELS, 128, 128), f),
            pltpu.VMEM((2, 2, 2, 128, 128), jnp.bfloat16),
            pltpu.VMEM((2 * G * R, 512), jnp.bfloat16),
            pltpu.VMEM((2 * G * R, 256), f),
            pltpu.VMEM((2, LEVELS, 136, 128), f),
            pltpu.SemaphoreType.DMA((blocks, LEVELS // G)),
            pltpu.SemaphoreType.DMA((2, blocks, LEVELS // G)),
            pltpu.SemaphoreType.DMA((blocks,)),
            pltpu.SemaphoreType.DMA((blocks,)),
            pltpu.SemaphoreType.DMA((8,)),
        ],
        compiler_params=pltpu.CompilerParams(vmem_limit_bytes=60 << 20),
        name="column_step",
    )(tracers, ec, nc, df, stencil_weights(), land, surf, pe, pw, south, north, ncs)
FIELDS = 5
CAP_ROWS = 48
SRC0 = 80
WGT0 = 128
LINK_ROWS = 176
MESH = pl.DeviceIdType.MESH


def exchange_kernel(tr_hbm, ec_hbm, nc_hbm, flux_hbm, src_hbm, wgt_hbm, tgt_hbm,
                    surf_hbm, pe_hbm, pw_hbm, south_hbm, north_hbm, ncs_hbm,
                    surf_ref, pe_ref, pw_ref, south_ref, north_ref, ncs_ref, T, EC, NC, flux_ref, src_ref, wgt_ref, tgt_ref,
                    L, RL, TG, WPa, WPb, TAa, TAb, TBa, TBb, Za, Zb, Ba, Bb, ACC, Q, pe_out, pw_out, rows_out, nc_out, load_sem, send_sem, recv_sem, out_sem):
    rows, cols = 128, 128
    lat, lon = lax.axis_index("lat"), lax.axis_index("lon")
    nlat, nlon = lax.axis_size("lat"), lax.axis_size("lon")
    north, south = lax.rem(lat + 1, nlat), lax.rem(lat + nlat - 1, nlat)
    east, west = lax.rem(lon + 1, nlon), lax.rem(lon + nlon - 1, nlon)

    loads = [
        pltpu.make_async_copy(src_hbm, src_ref, load_sem.at[0]),
        pltpu.make_async_copy(wgt_hbm, wgt_ref, load_sem.at[1]),
        pltpu.make_async_copy(flux_hbm, flux_ref, load_sem.at[2]),
        pltpu.make_async_copy(tgt_hbm, tgt_ref, load_sem.at[3]),
        pltpu.make_async_copy(tr_hbm, T, load_sem.at[4]),
        pltpu.make_async_copy(ec_hbm, EC, load_sem.at[5]),
        pltpu.make_async_copy(nc_hbm.at[:, rows - 8:rows, :], NC, load_sem.at[6]),
    ]
    for c in loads:
        c.start()

    barrier = pltpu.get_barrier_semaphore()
    for peer in ((lat, east), (lat, west), (north, lon), (south, lon), (north, east), (south, west)):
        pl.semaphore_signal(barrier, inc=1, device_id=peer, device_id_type=MESH)

    for c in loads[:4]:
        c.wait()
    field = lax.broadcasted_iota(jnp.int32, (8, cols), 0)
    for n in range(4):
        for h in range(16):
            lanes = pl.ds(n * 2048 + h * 128, 128)
            tile = flux_ref[0:6, lanes]
            more = jnp.where(field[0:5] == 1, jnp.broadcast_to(tile[5:6], (5, cols)), 0.0)
            L[n, h * FIELDS:(h + 1) * FIELDS, :] = tile[0:5] + more
        for j in range(CAP_ROWS):
            lanes = pl.ds(j * 128, 128)
            L[n, SRC0 + j:SRC0 + j + 1, :] = (src_ref[0, n:n + 1, lanes] - n * 2048).astype(jnp.float32)
            L[n, WGT0 + j:WGT0 + j + 1, :] = wgt_ref[0, n:n + 1, lanes]
            TG[n, j:j + 1, :] = tgt_ref[0, n:n + 1, lanes]

    b16 = jnp.bfloat16
    sub16 = lax.broadcasted_iota(jnp.int32, (16, cols), 0).astype(jnp.float32)
    subs = [(sub16 + 16.0 * s).astype(b16) for s in range(16)]
    one, zero16 = jnp.ones((16, cols), b16), jnp.zeros((16, cols), b16)

    def pick(n, box, WP, TA, TB, g):
        exists = jnp.where(lat >= n // 2, 1.0, 0.0)
        at = pl.ds(pl.multiple_of(g * 8, 8), 8)
        target = TG[n, at, :]
        row = (target >> 7) & 63
        TA[at, :] = (row >> 2).astype(jnp.float32)
        TB[at, :] = (((row & 3) << 6) + (target & 63)).astype(jnp.float32)
        cell = box[pl.ds(pl.multiple_of(SRC0 + g * 8, 8), 8), :].astype(jnp.int32)
        weight = box[pl.ds(pl.multiple_of(WGT0 + g * 8, 8), 8), :] * exists
        low = cell & 127
        high = cell >> 7
        for f in range(FIELDS):
            got = jnp.zeros((8, cols), jnp.float32)
            for h in range(16):
                line = jnp.broadcast_to(box[h * FIELDS + f:h * FIELDS + f + 1, :], (8, cols))
                got = jnp.where(high == h, jnp.take_along_axis(line, low, axis=1), got)
            got = got * weight
            top = got.astype(b16).astype(jnp.float32)
            WP[f, at, :] = top
            WP[FIELDS + f, at, :] = got - top

    def hot(WP, TA, TB, Z, B, g):
        for u in range(8):
            j = g * 8 + u
            lanes = pl.ds(pl.multiple_of(j * 128, 128), 128)
            a = jnp.broadcast_to(TA[pl.ds(j, 1), :], (16, cols)).astype(b16) == subs[0]
            b = jnp.broadcast_to(TB[pl.ds(j, 1), :], (16, cols)).astype(b16)
            for w in range(2 * FIELDS):
                v = jnp.broadcast_to(WP[w, pl.ds(j, 1), :], (16, cols)).astype(b16)
                Z[w * 16:(w + 1) * 16, lanes] = jnp.where(a, v, zero16)
            for s in range(16):
                B[s * 16:(s + 1) * 16, lanes] = jnp.where(b == subs[s], one, zero16)

    def place(Z, B, g):
        size = CAP_ROWS * 128
        lanes = pl.ds(pl.multiple_of(g * size, size), size)
        return lax.dot_general(Z[:, lanes], B[:, lanes], (((1,), (1,)), ((), ())), preferred_element_type=jnp.float32)

    def spread(n):
        col0 = (1 - n % 2) * 64
        for f in range(FIELDS):
            total = ACC[f * 16:(f + 1) * 16, :] + ACC[(FIELDS + f) * 16:(FIELDS + f + 1) * 16, :]
            for i in range(4):
                part = total[:, (i // 2) * 128:(i // 2 + 1) * 128]
                if (i % 2) * 64 != col0:
                    part = pltpu.roll(part, 64, 1)
                Q[n, f, i] = part

    order = (0, 2, 1, 3)
    boxes = {0: L.at[0], 1: RL.at[0], 2: RL.at[1], 3: RL.at[2]}
    words = ((WPa, TAa, TBa), (WPb, TAb, TBb))
    hots = ((Za, Ba), (Zb, Bb))

    def stage(picked, hotted, placed):
        def body(g, carry):
            if placed is not None:
                ACC[...] = place(*hots[placed % 2], g)
            for v in range(CAP_ROWS // 8):
                if hotted is not None:
                    hot(*words[hotted % 2], *hots[hotted % 2], v)
                if picked is not None:
                    pick(order[picked], boxes[order[picked]], *words[picked % 2], v)
            return carry

        lax.fori_loop(0, 1, body, 0)
        if placed is not None:
            spread(order[placed])

    stage(0, None, None)
    stage(None, 0, None)

    pl.semaphore_wait(barrier, 6)

    def send(src, dst, at, peer):
        copy = pltpu.make_async_remote_copy(
            src_ref=src, dst_ref=dst, send_sem=send_sem.at[at], recv_sem=recv_sem.at[at],
            device_id=peer, device_id_type=MESH)
        copy.start()
        return copy

    links = {
        1: send(L.at[1], RL.at[0], 0, (lat, east)),
        2: send(L.at[2], RL.at[1], 1, (north, lon)),
        3: send(L.at[3], RL.at[2], 2, (north, east)),
    }


    for c in loads[4:]:
        c.wait()
    lane = lax.broadcasted_iota(jnp.int32, (64, cols), 1)
    for t in range(2):
        for z in range(2):
            rr = pl.ds(z * 64, 64)

            def pack(q, carry):
                pe, pw = carry
                for u in range(8):
                    k = q * 8 + u
                    half = k // HALF
                    j = k - half * HALF
                    by = 4 * j + 2 * (1 - half)
                    y = pltpu.roll(T[t, k, rr, :], by, 1)
                    off = (lane - by) & 127
                    pe = jnp.where(off < 2, y, pe)
                    pw = jnp.where(off >= 126, y, pw)
                return pe, pw

            zero = jnp.zeros((64, cols), jnp.float32)
            pe, pw = lax.fori_loop(0, LEVELS // 8, pack, (zero, zero))

            def pack_courant(q, pw):
                for u in range(8):
                    j = q * 8 + u
                    y = pltpu.roll(EC[t * HALF + j, rr, :], j + 97, 1)
                    pw = jnp.where(lane == 96 + j, y, pw)
                return pw

            pw = lax.fori_loop(0, HALF // 8, pack_courant, pw)
            pe_out[t, rr, :] = pe
            pw_out[t, rr, :] = pw

    def edge_rows(k, carry):
        for t in range(2):
            rows_out[0, t, k] = T[t, k, 0:2, :]
            rows_out[1, t, k] = T[t, k, rows - 2:rows, :]
        nc_out[k] = NC[k, 7:8, :]
        return carry

    lax.fori_loop(0, LEVELS, edge_rows, 0)

    halos = [
        send(pe_out, pe_ref, 3, (lat, west)),
        send(pw_out, pw_ref, 4, (lat, east)),
        send(rows_out.at[0], north_ref, 5, (south, lon)),
        send(rows_out.at[1], south_ref, 6, (north, lon)),
        send(nc_out, ncs_ref, 7, (north, lon)),
    ]

    links[order[1]].wait()
    stage(1, None, 0)
    links[order[2]].wait()
    stage(2, 1, None)
    links[order[3]].wait()
    stage(3, 2, 1)
    stage(None, 3, 2)
    for c in halos:
        c.wait()
    below = jnp.where(lat > 0, 1.0, 0.0)
    over = jnp.where(lat < nlat - 1, 1.0, 0.0)
    south_ref[...] = south_ref[...] * below
    ncs_ref[...] = ncs_ref[...] * below
    north_ref[...] = north_ref[...] * over
    results = [
        pltpu.make_async_copy(v, h, out_sem.at[p]) for p, (v, h) in enumerate((
            (pe_ref, pe_hbm), (pw_ref, pw_hbm), (south_ref, south_hbm), (north_ref, north_hbm), (ncs_ref, ncs_hbm),
            (surf_ref, surf_hbm)))
    ]
    for c in results[:5]:
        c.start()

    stage(None, None, 3)

    left = lax.broadcasted_iota(jnp.int32, (16, cols), 1) < 64
    for a in range(2):
        for f in range(FIELDS):
            for i in range(4):
                surf_ref[f, pl.ds((1 - a) * 64 + i, 16, stride=4), :] = jnp.where(left, Q[2 * a + 1, f, i], Q[2 * a, f, i])
    results[5].start()
    for c in results:
        c.wait()


def exchange(tracers, ec, nc, fluxes, source_cell, link_weight, target_cell):
    hbm = pl.BlockSpec(memory_space=pltpu.HBM)
    f = jnp.float32
    s = jax.ShapeDtypeStruct
    return pl.pallas_call(
        exchange_kernel,
        out_shape=[s((FIELDS, 128, 128), f), s((2, 128, 128), f), s((2, 128, 128), f), s((2, LEVELS, 2, 128), f),
                   s((2, LEVELS, 2, 128), f), s((LEVELS, 1, 128), f)],
        in_specs=[hbm] * 7,
        out_specs=[hbm] * 6,
        scratch_shapes=[
            pltpu.VMEM((FIELDS, 128, 128), f),
            pltpu.VMEM((2, 128, 128), f),
            pltpu.VMEM((2, 128, 128), f),
            pltpu.VMEM((2, LEVELS, 2, 128), f),
            pltpu.VMEM((2, LEVELS, 2, 128), f),
            pltpu.VMEM((LEVELS, 1, 128), f),
            pltpu.VMEM((2, LEVELS, 128, 128), f),
            pltpu.VMEM((LEVELS, 128, 128), f),
            pltpu.VMEM((LEVELS, 8, 128), f),
            pltpu.VMEM((6, 8192), f),
            pltpu.VMEM((1, 4, 6144), jnp.int32),
            pltpu.VMEM((1, 4, 6144), f),
            pltpu.VMEM((1, 4, 6144), jnp.int32),
            pltpu.VMEM((4, LINK_ROWS, 128), f),
            pltpu.VMEM((3, LINK_ROWS, 128), f),
            pltpu.VMEM((4, CAP_ROWS, 128), jnp.int32),
            pltpu.VMEM((2 * FIELDS, CAP_ROWS, 128), f),
            pltpu.VMEM((2 * FIELDS, CAP_ROWS, 128), f),
            pltpu.VMEM((CAP_ROWS, 128), f),
            pltpu.VMEM((CAP_ROWS, 128), f),
            pltpu.VMEM((CAP_ROWS, 128), f),
            pltpu.VMEM((CAP_ROWS, 128), f),
            pltpu.VMEM((2 * FIELDS * 16, 6144), jnp.bfloat16),
            pltpu.VMEM((2 * FIELDS * 16, 6144), jnp.bfloat16),
            pltpu.VMEM((256, 6144), jnp.bfloat16),
            pltpu.VMEM((256, 6144), jnp.bfloat16),
            pltpu.VMEM((2 * FIELDS * 16, 256), f),
            pltpu.VMEM((4, FIELDS, 4, 16, 128), f),
            pltpu.VMEM((2, 128, 128), f),
            pltpu.VMEM((2, 128, 128), f),
            pltpu.VMEM((2, 2, LEVELS, 2, 128), f),
            pltpu.VMEM((LEVELS, 1, 128), f),
            pltpu.SemaphoreType.DMA((7,)),
            pltpu.SemaphoreType.DMA((8,)),
            pltpu.SemaphoreType.DMA((8,)),
            pltpu.SemaphoreType.DMA((6,)),
        ],
        compiler_params=pltpu.CompilerParams(collective_id=0, has_side_effects=True, vmem_limit_bytes=60 << 20),
        name="exchange",
    )(tracers, ec, nc, fluxes, source_cell, link_weight, target_cell)


def local(tracers, east_courant, north_courant, diffusivity, land_sea, fluxes, source_cell, link_weight, target_cell):
    surf, pe, pw, south, north, ncs = exchange(
        tracers, east_courant, north_courant, fluxes, source_cell, link_weight, target_cell)
    return column_step(tracers, east_courant, north_courant, diffusivity, land_sea, surf, pe, pw, south, north, ncs)


def solution(mesh):
    in_specs = (
        P(None, None, "lat", "lon"),
        P(None, "lat", "lon"),
        P(None, "lat", "lon"),
        P(None, "lat", "lon"),
        P("lat", "lon"),
        P(None, ("lat", "lon")),
        P(("lat", "lon"), None, None),
        P(("lat", "lon"), None, None),
        P(("lat", "lon"), None, None),
    )
    out_specs = P(None, None, "lat", "lon")
    return jax.shard_map(local, mesh=mesh, in_specs=in_specs, out_specs=out_specs, check_vma=False)
```

```python
import math
import jax, jax.numpy as jnp
import numpy as np
from jax import lax
from jax.experimental import pallas as pl
from jax.experimental.pallas import tpu as pltpu
from jax.sharding import PartitionSpec as P

LEVELS = 48
HALF = 24
R = 32
G = 12
PAD = 8


def stencil_weights():
    cols = 128
    main = np.zeros((cols, 2 * cols), np.float32)
    for i in range(cols):
        for off, w in ((-1, -1), (0, 7), (1, 7), (2, -1)):
            if 0 <= i + off < cols:
                main[i + off, i] = w
        for off, w in ((-2, -1), (-1, 7), (0, 7), (1, -1)):
            if 0 <= i + off < cols:
                main[i + off, cols + i] = w
    halves = []
    for half in range(2):
        edge = np.zeros((cols, 2 * cols), np.float32)
        order = (-2, -1, 128, 129) if half == 0 else (128, 129, -2, -1)
        for lane in range(cols):
            p = order[lane % 4]
            for i in range(cols):
                edge[lane, i] = {-1: -1, 0: 7, 1: 7, 2: -1}.get(p - i, 0)
                edge[lane, cols + i] = {-2: -1, -1: 7, 0: 7, 1: -1}.get(p - i, 0)
        halves.append(np.concatenate([main, main, edge, edge], 0))
    return jnp.asarray(np.stack(halves), jnp.bfloat16)


def two_pieces(x):
    high = x.astype(jnp.bfloat16)
    return high, (x - high.astype(jnp.float32)).astype(jnp.bfloat16)


def column_kernel(tr_hbm, ec_hbm, nc_hbm, df_hbm, w_hbm, land_hbm, surf_hbm, pe_hbm, pw_hbm, south_hbm, north_hbm, ncs_hbm,
                  out_hbm, w_ref, land_ref, surf_ref, pe_ref, pw_ref, south_ref, north_ref, ncs_ref, T, EC, NC, DF, C, OUT, H, X, S, FN, tr_sem, co_sem, df_sem, out_sem, small_sem):
    rows, cols = 128, 128
    blocks = rows // R

    groups = LEVELS // G

    def span(i, size):
        return pl.ds(pl.multiple_of(i * size, size), size)

    def load_tracers(b, g):
        return pltpu.make_async_copy(
            tr_hbm.at[:, span(g, G), span(b, R), :],
            T.at[:, span(g, G), pl.ds(pl.multiple_of(b * R + PAD, PAD), R), :], tr_sem.at[b, g])

    def load_courants(b, g):
        return [pltpu.make_async_copy(h.at[span(g, G), span(b, R), :], v.at[span(g, G), span(b, R), :], co_sem.at[p, b, g])
                for p, (h, v) in enumerate(((ec_hbm, EC), (nc_hbm, NC)))]

    def load_diffusivity(b):
        return pltpu.make_async_copy(df_hbm.at[:, span(b, R), :], DF.at[:, span(b, R), :], df_sem.at[b])

    def start_block(b, carry):
        def start_group(g, carry):
            @pl.when(b == 0)
            def _():
                load_tracers(0, g).start()

            @pl.when(b + 1 < blocks)
            def _():
                load_tracers(b + 1, g).start()

            for c in load_courants(b, g):
                c.start()
            return carry

        lax.fori_loop(0, groups, start_group, 0)
        load_diffusivity(b).start()
        return carry

    small = [
        pltpu.make_async_copy(h, v, small_sem.at[p]) for p, (h, v) in enumerate((
            (pe_hbm, pe_ref), (pw_hbm, pw_ref), (south_hbm, south_ref), (north_hbm, north_ref), (ncs_hbm, ncs_ref),
            (w_hbm, w_ref), (surf_hbm, surf_ref), (land_hbm, land_ref)))
    ]
    for c in small[:6]:
        c.start()
    start_block(0, 0)
    for c in small[6:]:
        c.start()
    lax.fori_loop(1, blocks, start_block, 0)
    for c in small[:6]:
        c.wait()

    lane = lax.broadcasted_iota(jnp.int32, (rows, cols), 1)
    low = lane % 4 < 2
    for t in range(2):
        pe, pw = pe_ref[t], pw_ref[t]
        for half in range(2):
            h = jnp.where(low, pw, pe) if half == 0 else jnp.where(low, pe, pw)
            H[t, half, 0], H[t, half, 1] = two_pieces(h)

    def pad_rows(q, carry):
        for u in range(8):
            k = q * 8 + u
            for t in range(2):
                T[t, k, PAD - 2:PAD, :] = south_ref[t, k]
                T[t, k, PAD + rows:PAD + rows + 2, :] = north_ref[t, k]
        return carry

    lax.fori_loop(0, LEVELS // 8, pad_rows, 0)

    def block(b, carry):
        r = pl.multiple_of(b * R, R)
        rr = pl.ds(r, R)
        lane = lax.broadcasted_iota(jnp.int32, (R, cols), 1)
        first = lane == 0

        for half in range(2):
            def group(q, carry):
                g = half * (HALF // G) + q

                @pl.when(b == 0)
                def _():
                    load_tracers(0, g).wait()

                @pl.when(b + 1 < blocks)
                def _():
                    load_tracers(b + 1, g).wait()

                for c in load_courants(b, g):
                    c.wait()

                @pl.when(b == 0)
                def _():
                    for u in range(G):
                        k = g * G + u
                        for t in range(2):
                            s = T[t, k, PAD - 2:PAD - 1, :] + T[t, k, PAD + 1:PAD + 2, :]
                            m = T[t, k, PAD - 1:PAD, :] + T[t, k, PAD:PAD + 1, :]
                            FN[t, k, PAD - 1:PAD, :] = ncs_ref[k] * (7.0 * m - s)

                for u in range(G):
                    j = q * G + u
                    k = half * HALF + j
                    here = ((lane + 2 * half) & (cols - 1)) >> 2 == j
                    for t in range(2):
                        x = T[t, k, pl.ds(r + PAD, R), :]
                        at = pl.ds((u * 2 + t) * R, R)
                        X[at, 0:cols], X[at, cols:2 * cols] = two_pieces(x)
                        for p in range(2):
                            h = H[t, half, p, rr, :]
                            X[at, (2 + p) * cols:(3 + p) * cols] = jnp.where(here, h, jnp.zeros_like(h))
                S[...] = jnp.dot(X[...], w_ref[half], preferred_element_type=jnp.float32)
                for u in range(G):
                    j = q * G + u
                    k = half * HALF + j
                    ce = EC[k, rr, :]
                    cn = NC[k, rr, :]
                    hec = pltpu.roll(pw_ref[half, rr, :], cols - 96 - j, 1)
                    cw = jnp.where(first, hec, pltpu.roll(ce, 1, 1))
                    for t in range(2):
                        at = pl.ds((u * 2 + t) * R, R)
                        x = T[t, k, pl.ds(r + PAD, R), :]
                        n1 = T[t, k, pl.ds(r + PAD + 1, R), :]
                        n2 = T[t, k, pl.ds(r + PAD + 2, R), :]
                        s1 = T[t, k, pl.ds(r + PAD - 1, R), :]
                        fn = cn * (7.0 * (x + n1) - (s1 + n2))
                        FN[t, k, pl.ds(r + PAD, R), :] = fn
                        fs = FN[t, k, pl.ds(r + PAD - 1, R), :]
                        div = (ce * S[at, 0:cols] - cw * S[at, cols:2 * cols]) + (fn - fs)
                        OUT[t, k, rr, :] = x - div * (1.0 / 12.0)
                return carry

            lax.fori_loop(0, HALF // G, group, 0)

        load_diffusivity(b).wait()

        @pl.when(b == 0)
        def _():
            for c in small[6:]:
                c.wait()

        stress = 2.0 * jnp.sqrt(surf_ref[3, rr, :] * surf_ref[3, rr, :] + surf_ref[4, rr, :] * surf_ref[4, rr, :])
        heat = 0.5 * surf_ref[2, rr, :]
        tops = [0.5 * surf_ref[0, rr, :], 0.5 * surf_ref[1, rr, :]]
        above = None
        cprev = None
        vprev = [None, None]
        for k in range(LEVELS):
            if k < LEVELS - 1:
                below = DF[k, rr, :] + stress * math.exp(-4.0 * k / LEVELS)
            absorb = math.exp(-4.0 * k / LEVELS) - math.exp(-4.0 * (k + 1) / LEVELS)
            adv = [OUT[0, k, rr, :] + heat * absorb, OUT[1, k, rr, :]]
            if k == 0:
                adv[0] = adv[0] + tops[0]
                adv[1] = adv[1] + tops[1]
                inv = 1.0 / (1.0 + below)
                v = [adv[0] * inv, adv[1] * inv]
            else:
                pivot = 1.0 + above * (1.0 - cprev)
                if k < LEVELS - 1:
                    pivot = pivot + below
                inv = 1.0 / pivot
                v = [(adv[t] + above * vprev[t]) * inv for t in range(2)]
            if k < LEVELS - 1:
                cprev = below * inv
                C[k] = cprev
                above = below
                for t in range(2):
                    OUT[t, k, rr, :] = v[t]
            vprev = v
        sea = land_ref[rr, :] == 1
        x = vprev
        for k in range(LEVELS - 1, -1, -1):
            if k < LEVELS - 1:
                c = C[k]
                x = [OUT[t, k, rr, :] + c * x[t] for t in range(2)]
            for t in range(2):
                OUT[t, k, rr, :] = jnp.where(sea, x[t], T[t, k, pl.ds(r + PAD, R), :])
        pltpu.make_async_copy(OUT.at[:, :, rr, :], out_hbm.at[:, :, rr, :], out_sem.at[b]).start()
        return carry

    lax.fori_loop(0, blocks, block, 0)

    def drain(b, carry):
        rr = pl.ds(pl.multiple_of(b * R, R), R)
        pltpu.make_async_copy(OUT.at[:, :, rr, :], out_hbm.at[:, :, rr, :], out_sem.at[b]).wait()
        return carry

    lax.fori_loop(0, blocks, drain, 0)


def column_step(tracers, ec, nc, df, land, surf, pe, pw, south, north, ncs):
    any_ = pl.BlockSpec(memory_space=pltpu.HBM)
    blocks = 128 // R
    f = jnp.float32
    return pl.pallas_call(
        column_kernel,
        out_shape=jax.ShapeDtypeStruct(tracers.shape, f),
        in_specs=[any_] * 12,
        out_specs=any_,
        scratch_shapes=[
            pltpu.VMEM((2, 512, 256), jnp.bfloat16),
            pltpu.VMEM((128, 128), jnp.int32),
            pltpu.VMEM((5, 128, 128), f),
            pltpu.VMEM((2, 128, 128), f),
            pltpu.VMEM((2, 128, 128), f),
            pltpu.VMEM((2, LEVELS, 2, 128), f),
            pltpu.VMEM((2, LEVELS, 2, 128), f),
            pltpu.VMEM((LEVELS, 1, 128), f),
            pltpu.VMEM((2, LEVELS, 144, 128), f),
            pltpu.VMEM((LEVELS, 128, 128), f),
            pltpu.VMEM((LEVELS, 128, 128), f),
            pltpu.VMEM((LEVELS, 128, 128), f),
            pltpu.VMEM((LEVELS, R, 128), f),
            pltpu.VMEM((2, LEVELS, 128, 128), f),
            pltpu.VMEM((2, 2, 2, 128, 128), jnp.bfloat16),
            pltpu.VMEM((2 * G * R, 512), jnp.bfloat16),
            pltpu.VMEM((2 * G * R, 256), f),
            pltpu.VMEM((2, LEVELS, 136, 128), f),
            pltpu.SemaphoreType.DMA((blocks, LEVELS // G)),
            pltpu.SemaphoreType.DMA((2, blocks, LEVELS // G)),
            pltpu.SemaphoreType.DMA((blocks,)),
            pltpu.SemaphoreType.DMA((blocks,)),
            pltpu.SemaphoreType.DMA((8,)),
        ],
        compiler_params=pltpu.CompilerParams(vmem_limit_bytes=60 << 20),
        name="column_step",
    )(tracers, ec, nc, df, stencil_weights(), land, surf, pe, pw, south, north, ncs)
FIELDS = 5
CAP_ROWS = 48
SRC0 = 80
WGT0 = 128
LINK_ROWS = 176
MESH = pl.DeviceIdType.MESH


def exchange_kernel(tr_hbm, ec_hbm, nc_hbm, flux_hbm, src_hbm, wgt_hbm, tgt_hbm,
                    surf_hbm, pe_hbm, pw_hbm, south_hbm, north_hbm, ncs_hbm,
                    surf_ref, pe_ref, pw_ref, south_ref, north_ref, ncs_ref, T, EC, NC, flux_ref, src_ref, wgt_ref, tgt_ref,
                    L, RL, TG, WPa, WPb, TAa, TAb, TBa, TBb, Za, Zb, Ba, Bb, ACC, Q, pe_out, pw_out, rows_out, nc_out, load_sem, send_sem, recv_sem, out_sem):
    rows, cols = 128, 128
    lat, lon = lax.axis_index("lat"), lax.axis_index("lon")
    nlat, nlon = lax.axis_size("lat"), lax.axis_size("lon")
    north, south = lax.rem(lat + 1, nlat), lax.rem(lat + nlat - 1, nlat)
    east, west = lax.rem(lon + 1, nlon), lax.rem(lon + nlon - 1, nlon)

    loads = [
        pltpu.make_async_copy(src_hbm, src_ref, load_sem.at[0]),
        pltpu.make_async_copy(wgt_hbm, wgt_ref, load_sem.at[1]),
        pltpu.make_async_copy(flux_hbm, flux_ref, load_sem.at[2]),
        pltpu.make_async_copy(tgt_hbm, tgt_ref, load_sem.at[3]),
        pltpu.make_async_copy(tr_hbm, T, load_sem.at[4]),
        pltpu.make_async_copy(ec_hbm, EC, load_sem.at[5]),
        pltpu.make_async_copy(nc_hbm.at[:, rows - 8:rows, :], NC, load_sem.at[6]),
    ]
    for c in loads:
        c.start()

    barrier = pltpu.get_barrier_semaphore()
    for peer in ((lat, east), (lat, west), (north, lon), (south, lon), (north, east), (south, west)):
        pl.semaphore_signal(barrier, inc=1, device_id=peer, device_id_type=MESH)

    for c in loads[:4]:
        c.wait()
    field = lax.broadcasted_iota(jnp.int32, (8, cols), 0)
    for n in range(4):
        for h in range(16):
            lanes = pl.ds(n * 2048 + h * 128, 128)
            tile = flux_ref[0:6, lanes]
            more = jnp.where(field[0:5] == 1, jnp.broadcast_to(tile[5:6], (5, cols)), 0.0)
            L[n, h * FIELDS:(h + 1) * FIELDS, :] = tile[0:5] + more
        for j in range(CAP_ROWS):
            lanes = pl.ds(j * 128, 128)
            L[n, SRC0 + j:SRC0 + j + 1, :] = (src_ref[0, n:n + 1, lanes] - n * 2048).astype(jnp.float32)
            L[n, WGT0 + j:WGT0 + j + 1, :] = wgt_ref[0, n:n + 1, lanes]
            TG[n, j:j + 1, :] = tgt_ref[0, n:n + 1, lanes]

    b16 = jnp.bfloat16
    sub16 = lax.broadcasted_iota(jnp.int32, (16, cols), 0).astype(jnp.float32)
    subs = [(sub16 + 16.0 * s).astype(b16) for s in range(16)]
    one, zero16 = jnp.ones((16, cols), b16), jnp.zeros((16, cols), b16)

    def pick(n, box, WP, TA, TB, g):
        exists = jnp.where(lat >= n // 2, 1.0, 0.0)
        at = pl.ds(pl.multiple_of(g * 8, 8), 8)
        target = TG[n, at, :]
        row = (target >> 7) & 63
        TA[at, :] = (row >> 2).astype(jnp.float32)
        TB[at, :] = (((row & 3) << 6) + (target & 63)).astype(jnp.float32)
        cell = box[pl.ds(pl.multiple_of(SRC0 + g * 8, 8), 8), :].astype(jnp.int32)
        weight = box[pl.ds(pl.multiple_of(WGT0 + g * 8, 8), 8), :] * exists
        low = cell & 127
        high = cell >> 7
        for f in range(FIELDS):
            got = jnp.zeros((8, cols), jnp.float32)
            for h in range(16):
                line = jnp.broadcast_to(box[h * FIELDS + f:h * FIELDS + f + 1, :], (8, cols))
                got = jnp.where(high == h, jnp.take_along_axis(line, low, axis=1), got)
            got = got * weight
            top = got.astype(b16).astype(jnp.float32)
            WP[f, at, :] = top
            WP[FIELDS + f, at, :] = got - top

    def hot(WP, TA, TB, Z, B, g):
        for u in range(8):
            j = g * 8 + u
            lanes = pl.ds(pl.multiple_of(j * 128, 128), 128)
            a = jnp.broadcast_to(TA[pl.ds(j, 1), :], (16, cols)).astype(b16) == subs[0]
            b = jnp.broadcast_to(TB[pl.ds(j, 1), :], (16, cols)).astype(b16)
            for w in range(2 * FIELDS):
                v = jnp.broadcast_to(WP[w, pl.ds(j, 1), :], (16, cols)).astype(b16)
                Z[w * 16:(w + 1) * 16, lanes] = jnp.where(a, v, zero16)
            for s in range(16):
                B[s * 16:(s + 1) * 16, lanes] = jnp.where(b == subs[s], one, zero16)

    def place(Z, B, g):
        size = CAP_ROWS * 128
        lanes = pl.ds(pl.multiple_of(g * size, size), size)
        return lax.dot_general(Z[:, lanes], B[:, lanes], (((1,), (1,)), ((), ())), preferred_element_type=jnp.float32)

    def spread(n):
        col0 = (1 - n % 2) * 64
        for f in range(FIELDS):
            total = ACC[f * 16:(f + 1) * 16, :] + ACC[(FIELDS + f) * 16:(FIELDS + f + 1) * 16, :]
            for i in range(4):
                part = total[:, (i // 2) * 128:(i // 2 + 1) * 128]
                if (i % 2) * 64 != col0:
                    part = pltpu.roll(part, 64, 1)
                Q[n, f, i] = part

    order = (0, 2, 1, 3)
    boxes = {0: L.at[0], 1: RL.at[0], 2: RL.at[1], 3: RL.at[2]}
    words = ((WPa, TAa, TBa), (WPb, TAb, TBb))
    hots = ((Za, Ba), (Zb, Bb))

    def stage(picked, hotted, placed):
        def body(g, carry):
            if placed is not None:
                ACC[...] = place(*hots[placed % 2], g)
            for v in range(CAP_ROWS // 8):
                if hotted is not None:
                    hot(*words[hotted % 2], *hots[hotted % 2], v)
                if picked is not None:
                    pick(order[picked], boxes[order[picked]], *words[picked % 2], v)
            return carry

        lax.fori_loop(0, 1, body, 0)
        if placed is not None:
            spread(order[placed])

    stage(0, None, None)
    stage(None, 0, None)

    pl.semaphore_wait(barrier, 6)

    def send(src, dst, at, peer):
        copy = pltpu.make_async_remote_copy(
            src_ref=src, dst_ref=dst, send_sem=send_sem.at[at], recv_sem=recv_sem.at[at],
            device_id=peer, device_id_type=MESH)
        copy.start()
        return copy

    links = {
        1: send(L.at[1], RL.at[0], 0, (lat, east)),
        2: send(L.at[2], RL.at[1], 1, (north, lon)),
        3: send(L.at[3], RL.at[2], 2, (north, east)),
    }


    for c in loads[4:]:
        c.wait()
    lane = lax.broadcasted_iota(jnp.int32, (64, cols), 1)
    for t in range(2):
        for z in range(2):
            rr = pl.ds(z * 64, 64)

            def pack(q, carry):
                pe, pw = carry
                for u in range(8):
                    k = q * 8 + u
                    half = k // HALF
                    j = k - half * HALF
                    by = 4 * j + 2 * (1 - half)
                    y = pltpu.roll(T[t, k, rr, :], by, 1)
                    off = (lane - by) & 127
                    pe = jnp.where(off < 2, y, pe)
                    pw = jnp.where(off >= 126, y, pw)
                return pe, pw

            zero = jnp.zeros((64, cols), jnp.float32)
            pe, pw = lax.fori_loop(0, LEVELS // 8, pack, (zero, zero))

            def pack_courant(q, pw):
                for u in range(8):
                    j = q * 8 + u
                    y = pltpu.roll(EC[t * HALF + j, rr, :], j + 97, 1)
                    pw = jnp.where(lane == 96 + j, y, pw)
                return pw

            pw = lax.fori_loop(0, HALF // 8, pack_courant, pw)
            pe_out[t, rr, :] = pe
            pw_out[t, rr, :] = pw

    columns = [
        send(pe_out, pe_ref, 3, (lat, west)),
        send(pw_out, pw_ref, 4, (lat, east)),
    ]

    def edge_rows(q, carry):
        for u in range(8):
            k = q * 8 + u
            for t in range(2):
                rows_out[0, t, k] = T[t, k, 0:2, :]
                rows_out[1, t, k] = T[t, k, rows - 2:rows, :]
            nc_out[k] = NC[k, 7:8, :]
        return carry

    lax.fori_loop(0, LEVELS // 8, edge_rows, 0)

    halos = [
        send(rows_out.at[0], north_ref, 5, (south, lon)),
        send(rows_out.at[1], south_ref, 6, (north, lon)),
        send(nc_out, ncs_ref, 7, (north, lon)),
    ]

    links[order[1]].wait()
    stage(1, None, 0)
    links[order[2]].wait()
    stage(2, 1, None)
    links[order[3]].wait()
    stage(3, 2, 1)
    stage(None, 3, 2)
    for c in columns + halos:
        c.wait()
    below = jnp.where(lat > 0, 1.0, 0.0)
    over = jnp.where(lat < nlat - 1, 1.0, 0.0)
    south_ref[...] = south_ref[...] * below
    ncs_ref[...] = ncs_ref[...] * below
    north_ref[...] = north_ref[...] * over
    results = [
        pltpu.make_async_copy(v, h, out_sem.at[p]) for p, (v, h) in enumerate((
            (pe_ref, pe_hbm), (pw_ref, pw_hbm), (south_ref, south_hbm), (north_ref, north_hbm), (ncs_ref, ncs_hbm),
            (surf_ref, surf_hbm)))
    ]
    for c in results[:5]:
        c.start()

    stage(None, None, 3)

    left = lax.broadcasted_iota(jnp.int32, (16, cols), 1) < 64
    for a in range(2):
        for f in range(FIELDS):
            for i in range(4):
                surf_ref[f, pl.ds((1 - a) * 64 + i, 16, stride=4), :] = jnp.where(left, Q[2 * a + 1, f, i], Q[2 * a, f, i])
    results[5].start()
    for c in results:
        c.wait()


def exchange(tracers, ec, nc, fluxes, source_cell, link_weight, target_cell):
    hbm = pl.BlockSpec(memory_space=pltpu.HBM)
    f = jnp.float32
    s = jax.ShapeDtypeStruct
    return pl.pallas_call(
        exchange_kernel,
        out_shape=[s((FIELDS, 128, 128), f), s((2, 128, 128), f), s((2, 128, 128), f), s((2, LEVELS, 2, 128), f),
                   s((2, LEVELS, 2, 128), f), s((LEVELS, 1, 128), f)],
        in_specs=[hbm] * 7,
        out_specs=[hbm] * 6,
        scratch_shapes=[
            pltpu.VMEM((FIELDS, 128, 128), f),
            pltpu.VMEM((2, 128, 128), f),
            pltpu.VMEM((2, 128, 128), f),
            pltpu.VMEM((2, LEVELS, 2, 128), f),
            pltpu.VMEM((2, LEVELS, 2, 128), f),
            pltpu.VMEM((LEVELS, 1, 128), f),
            pltpu.VMEM((2, LEVELS, 128, 128), f),
            pltpu.VMEM((LEVELS, 128, 128), f),
            pltpu.VMEM((LEVELS, 8, 128), f),
            pltpu.VMEM((6, 8192), f),
            pltpu.VMEM((1, 4, 6144), jnp.int32),
            pltpu.VMEM((1, 4, 6144), f),
            pltpu.VMEM((1, 4, 6144), jnp.int32),
            pltpu.VMEM((4, LINK_ROWS, 128), f),
            pltpu.VMEM((3, LINK_ROWS, 128), f),
            pltpu.VMEM((4, CAP_ROWS, 128), jnp.int32),
            pltpu.VMEM((2 * FIELDS, CAP_ROWS, 128), f),
            pltpu.VMEM((2 * FIELDS, CAP_ROWS, 128), f),
            pltpu.VMEM((CAP_ROWS, 128), f),
            pltpu.VMEM((CAP_ROWS, 128), f),
            pltpu.VMEM((CAP_ROWS, 128), f),
            pltpu.VMEM((CAP_ROWS, 128), f),
            pltpu.VMEM((2 * FIELDS * 16, 6144), jnp.bfloat16),
            pltpu.VMEM((2 * FIELDS * 16, 6144), jnp.bfloat16),
            pltpu.VMEM((256, 6144), jnp.bfloat16),
            pltpu.VMEM((256, 6144), jnp.bfloat16),
            pltpu.VMEM((2 * FIELDS * 16, 256), f),
            pltpu.VMEM((4, FIELDS, 4, 16, 128), f),
            pltpu.VMEM((2, 128, 128), f),
            pltpu.VMEM((2, 128, 128), f),
            pltpu.VMEM((2, 2, LEVELS, 2, 128), f),
            pltpu.VMEM((LEVELS, 1, 128), f),
            pltpu.SemaphoreType.DMA((7,)),
            pltpu.SemaphoreType.DMA((8,)),
            pltpu.SemaphoreType.DMA((8,)),
            pltpu.SemaphoreType.DMA((6,)),
        ],
        compiler_params=pltpu.CompilerParams(collective_id=0, has_side_effects=True, vmem_limit_bytes=60 << 20),
        name="exchange",
    )(tracers, ec, nc, fluxes, source_cell, link_weight, target_cell)


def local(tracers, east_courant, north_courant, diffusivity, land_sea, fluxes, source_cell, link_weight, target_cell):
    surf, pe, pw, south, north, ncs = exchange(
        tracers, east_courant, north_courant, fluxes, source_cell, link_weight, target_cell)
    return column_step(tracers, east_courant, north_courant, diffusivity, land_sea, surf, pe, pw, south, north, ncs)


def solution(mesh):
    in_specs = (
        P(None, None, "lat", "lon"),
        P(None, "lat", "lon"),
        P(None, "lat", "lon"),
        P(None, "lat", "lon"),
        P("lat", "lon"),
        P(None, ("lat", "lon")),
        P(("lat", "lon"), None, None),
        P(("lat", "lon"), None, None),
        P(("lat", "lon"), None, None),
    )
    out_specs = P(None, None, "lat", "lon")
    return jax.shard_map(local, mesh=mesh, in_specs=in_specs, out_specs=out_specs, check_vma=False)
```
